32 devices in a mesh: seq: 8 (over z, x), head: 4 (over y, core).
Axes of the slice: x: 2, y: 2, z: 4, core: 2. Of those that a mesh axis runs over, the one named last changes fastest.
Arguments:
- queries: bfloat16 [1024, 4096], P('seq', 'head'), may hold values from -6 to 6
- keys: bfloat16 [1024, 4096], P('seq', 'head'), may hold values from -6 to 6
- values: bfloat16 [1024, 4096], P('seq', 'head'), may hold values from -3 to 3
- decay_codes: int32 [1024, 32], P('seq', 'head'), may hold values from 0 to 2048
- out_weight: bfloat16 [4096, 3072], P('head'), may hold values from -0.09375 to 0.09375
- out_grad: bfloat16 [1024, 3072], P('seq', 'head'), may hold values from -6 to 6
Outputs:
- mixed: bfloat16 [1024, 3072], P('seq', 'head')
- query_gradient: bfloat16 [1024, 4096], P('seq', 'head')
- key_grad: bfloat16 [1024, 4096], P('seq', 'head')
- value_gradient: bfloat16 [1024, 4096], P('seq', 'head')
The draws below stay inside these ranges and needn't reach their ends.
All inputs are finite; a program needn't handle non-finite values.
Results may differ from the reference program's by a relative error of at most 0.014.
Values may be sent and summed in bfloat16 or wider, within the bound.
No kernel may reach another device: no remote copies, remote signals or barrier semaphores. Data moves between devices by JAX's collectives and lax.ppermute only.
A program may use at most 128 MiB of HBM per device.

```python
import jax
import jax.numpy as jnp
from jax import lax

D = 3072
HEADS = 32
HEAD_DIM = 128
TOK_DEV = 128
TOKENS = 1024


def draw_decay_codes(key, part):
    keys_all = jax.random.split(key, 5)
    order = jax.random.permutation(keys_all[0], HEADS)
    slow_heads = order < HEADS // 2
    quick_decay_labels = jax.random.randint(keys_all[1], (TOKENS, HEADS), 100, 134)
    block_place = jnp.arange(TOKENS) // TOK_DEV
    head_offset = jax.random.randint(keys_all[4], (HEADS,), 0, 8)
    quick_block = (block_place[:, None] + head_offset[None, :]) % 8 == 0
    quick_here = jnp.logical_and(quick_block, jnp.logical_not(slow_heads)[None, :])
    baseline_decay_labels = jnp.where(quick_here, quick_decay_labels, 0)
    segment_places = jax.random.randint(keys_all[2], (3, HEADS), 0, TOKENS)
    nesting_level = jax.random.randint(keys_all[3], (3, HEADS), 820, 2049)
    nesting_level = nesting_level.at[0, 0].set(2048)
    token_places = jnp.arange(TOKENS)[:, None, None]
    segment_span = jnp.max(jnp.where(token_places == segment_places[None], nesting_level[None], 0), axis=1)
    return jnp.maximum(baseline_decay_labels, segment_span).astype(jnp.int32)


def level_of(own_key, extent, cuts, least, high):
    gain, own = 1.0, jax.random.fold_in(own_key, 6)
    for position, parts in cuts:
        heights = jnp.exp(jax.random.uniform(jax.random.fold_in(own, position), (parts,), jnp.float32, least / len(cuts), high / len(cuts)))
        gain = gain * jnp.repeat(heights, extent[position] // parts).reshape([-1 if axis == position else 1 for axis in range(len(extent))])
    return gain


def centred(key, extent, width, reach, pieces=(), dtype=jnp.bfloat16):
    gain = level_of(key, extent, pieces, -0.22, 0.18) if pieces else 1.0
    entries = jax.random.normal(key, extent, jnp.float32) * width * gain
    return jnp.minimum(jnp.maximum(entries, -reach), reach).astype(dtype)


def setup_inputs(seed: int = 0) -> dict:
    streams_of = jax.random.split(jax.random.key(seed), 7)
    return {
        "queries": centred(streams_of[0], (TOKENS, HEADS * HEAD_DIM), 1.0, 6.0, ((0, 8), (1, 4))),
        "keys": centred(streams_of[1], (TOKENS, HEADS * HEAD_DIM), 1.0, 6.0, ((0, 8), (1, 4))),
        "values": centred(streams_of[2], (TOKENS, HEADS * HEAD_DIM), 0.5, 3.0, ((0, 8), (1, 4))),
        "decay_codes": draw_decay_codes(jax.random.fold_in(streams_of[6], 71), 0),
        "out_weight": centred(streams_of[4], (HEADS * HEAD_DIM, D), (HEADS * HEAD_DIM) ** -0.5, 0.09375, ((0, 4),)),
        "out_grad": centred(streams_of[5], (TOKENS, D), 1.0, 6.0, ((0, 8), (1, 4))),
    }


def block_mask(cum_log):
    block_len = cum_log.shape[0]
    log_gap = cum_log.T[:, :, None] - cum_log.T[:, None, :]
    lower_part = (jnp.arange(block_len)[:, None] >= jnp.arange(block_len)[None, :])[None]
    return jnp.where(lower_part, jnp.exp(jnp.where(lower_part, log_gap, 0.0)), 0.0)


def factors(code_block):
    cum_log = jnp.cumsum(jnp.log(1.0 - code_block.astype(jnp.float32) / 4096.0), axis=0)
    rise_decay = jnp.exp(cum_log)
    fall_decay = jnp.exp(cum_log[-1][None, :] - cum_log)
    total_decay = jnp.exp(cum_log[-1])
    return block_mask(cum_log), rise_decay, fall_decay, total_decay


def local_terms(query_h, key_h, value_h, grad_h, code_block):
    att_scale = 1.0 / HEAD_DIM
    decay_mask, rise_decay, fall_decay, total_decay = factors(code_block)
    query_f = query_h.astype(jnp.float32)
    key_f = key_h.astype(jnp.float32)
    value_f = value_h.astype(jnp.float32)
    grad_f = grad_h.astype(jnp.float32)
    scores = jnp.einsum('she,the->hst', query_f, key_f)
    attn = (att_scale * scores * decay_mask).astype(jnp.bfloat16)
    pscores = jnp.einsum('she,the->hst', grad_f, value_f)
    pmat = (att_scale * pscores * decay_mask).astype(jnp.bfloat16)
    q_rise = (att_scale * rise_decay[:, :, None] * query_f).astype(jnp.bfloat16)
    g_rise = (att_scale * rise_decay[:, :, None] * grad_f).astype(jnp.bfloat16)
    k_fall = (fall_decay[:, :, None] * key_f).astype(jnp.bfloat16)
    v_fall = (fall_decay[:, :, None] * value_f).astype(jnp.bfloat16)
    return attn, pmat, q_rise, g_rise, k_fall, v_fall, total_decay


def reference(queries, keys, values, decay_codes, out_weight, out_grad):
    blocks = TOKENS // TOK_DEV
    grad_out = jnp.dot(out_grad, out_weight.T, preferred_element_type=jnp.float32).astype(jnp.bfloat16)

    def to_heads(array):
        return array.reshape(blocks, TOK_DEV, HEADS, HEAD_DIM)

    inputs = (to_heads(queries), to_heads(keys), to_heads(values), to_heads(grad_out),
              decay_codes.reshape(blocks, TOK_DEV, HEADS))

    def forward(state_in, block_item):
        query_h, key_h, value_h, grad_h, code_block = block_item
        attn, pmat, q_rise, g_rise, k_fall, v_fall, total_decay = local_terms(query_h, key_h, value_h, grad_h, code_block)
        state_b = state_in.astype(jnp.bfloat16).astype(jnp.float32)
        attn_out = jnp.einsum('hst,the->she', attn.astype(jnp.float32), value_h.astype(jnp.float32))
        attn_out = attn_out + jnp.einsum('shd,hde->she', q_rise.astype(jnp.float32), state_b)
        query_gradient = jnp.einsum('hst,thd->shd', pmat.astype(jnp.float32), key_h.astype(jnp.float32))
        query_gradient = query_gradient + jnp.einsum('she,hde->shd', g_rise.astype(jnp.float32), state_b)
        summary = jnp.einsum('thd,the->hde', k_fall.astype(jnp.float32), value_h.astype(jnp.float32))
        state_next = total_decay[:, None, None] * state_in + summary
        return state_next, (attn_out.astype(jnp.bfloat16), query_gradient.astype(jnp.bfloat16))

    def backward(carried, block_item):
        query_h, key_h, value_h, grad_h, code_block = block_item
        attn, pmat, q_rise, g_rise, k_fall, v_fall, total_decay = local_terms(query_h, key_h, value_h, grad_h, code_block)
        carry_b = carried.astype(jnp.bfloat16).astype(jnp.float32)
        key_grad = jnp.einsum('hst,shd->thd', pmat.astype(jnp.float32), query_h.astype(jnp.float32))
        key_grad = key_grad + jnp.einsum('the,hde->thd', v_fall.astype(jnp.float32), carry_b)
        value_gradient = jnp.einsum('hst,she->the', attn.astype(jnp.float32), grad_h.astype(jnp.float32))
        value_gradient = value_gradient + jnp.einsum('thd,hde->the', k_fall.astype(jnp.float32), carry_b)
        summary = jnp.einsum('shd,she->hde', q_rise.astype(jnp.float32), grad_h.astype(jnp.float32))
        carry_next = total_decay[:, None, None] * carried + summary
        return carry_next, (key_grad.astype(jnp.bfloat16), value_gradient.astype(jnp.bfloat16))

    zero_state = jnp.zeros((HEADS, HEAD_DIM, HEAD_DIM), jnp.float32)
    state_end, (attn_out, query_gradient) = lax.scan(forward, zero_state, inputs)
    carry_end, (key_grad, value_gradient) = lax.scan(backward, zero_state, inputs, reverse=True)
    width_all = HEADS * HEAD_DIM
    attn_flat = attn_out.reshape(TOKENS, width_all)
    mixed = jnp.dot(attn_flat, out_weight, preferred_element_type=jnp.float32).astype(jnp.bfloat16)
    return (mixed, query_gradient.reshape(TOKENS, width_all), key_grad.reshape(TOKENS, width_all),
            value_gradient.reshape(TOKENS, width_all))
```

```python
import functools

import jax
import jax.numpy as jnp
from jax import lax
from jax.experimental import pallas as pl
from jax.experimental.pallas import tpu as pltpu
from jax.sharding import PartitionSpec as P

F32 = jnp.float32
BF16 = jnp.bfloat16
VMEM = pl.BlockSpec(memory_space=pltpu.VMEM)
SMEM = pl.BlockSpec(memory_space=pltpu.SMEM)
HBM = pl.BlockSpec(memory_space=pl.ANY)


def dot(a, b, ca, cb):
    return lax.dot_general(a, b, (((ca,), (cb,)), ((), ())), preferred_element_type=F32)


def aligned(index, size):
    return pl.ds(pl.multiple_of(index * size, size), size)


def call(kernel, outs, specs, args, scratch=(), limit=16, flops=0, nbytes=0):
    return pl.pallas_call(
        kernel,
        out_shape=outs,
        in_specs=specs,
        out_specs=[VMEM] * len(outs),
        scratch_shapes=list(scratch),
        compiler_params=pltpu.CompilerParams(vmem_limit_bytes=limit << 20),
        cost_estimate=pl.CostEstimate(flops=flops, bytes_accessed=nbytes, transcendentals=0),
    )(*args)


def shape(dims, dtype):
    return jax.ShapeDtypeStruct(dims, dtype)


def running_log(codes, axis):
    total = jnp.log(1.0 - codes.astype(F32) / 4096.0)
    place = lax.broadcasted_iota(jnp.int32, total.shape, axis)
    step = 1
    while step < total.shape[axis]:
        total = total + jnp.where(place >= step, pltpu.roll(total, step, axis), 0.0)
        step *= 2
    return total


class Plan:
    def __init__(self, tok, heads, width, seq):
        self.tok, self.heads, self.width, self.seq = tok, heads, width, seq
        self.group = next(g for g in (4, 2, 1) if heads % g == 0 and seq % g == 0)
        self.groups = seq // self.group
        self.quarter = heads // self.group
        self.half_tail = 8 * pl.cdiv(self.quarter, 8)
        self.tail = 2 * self.half_tail
        self.body = self.quarter * width
        self.rows = self.body + self.tail


def tail_rows(plan, totals):
    place = lax.broadcasted_iota(jnp.int32, (plan.tail, plan.width), 0)
    rows = jnp.zeros((plan.tail, plan.width), F32)
    for i, total in enumerate(totals):
        high = total.astype(BF16).astype(F32)
        rows = jnp.where(place == i, high, rows)
        rows = jnp.where(place == plan.half_tail + i, total - high, rows)
    return rows


def read_tail(plan, ref, base, i):
    at = base + plan.body + i
    return ref[at : at + 1, :] + ref[at + plan.half_tail : at + plan.half_tail + 1, :]


def put_summaries(plan, rank, left, right, cum, outs, scratch):
    width = plan.width
    last = jnp.exp(cum[plan.tok - 1 : plan.tok, :])
    for q in range(plan.group):
        base = q * plan.rows
        totals = []
        for i in range(plan.quarter):
            h = q * plan.quarter + i
            scratch[base + i * width : base + (i + 1) * width, :] = dot(left(h), right(h), 0, 0)
            totals.append(jnp.broadcast_to(last[:, h : h + 1], (1, width)))
        scratch[base + plan.body : base + plan.rows, :] = tail_rows(plan, totals)
    outs[0][...] = scratch[aligned(rank, plan.rows), :]
    for j in range(1, plan.group):
        outs[j][...] = scratch[aligned(rank ^ j, plan.rows), :].astype(BF16)


def summary_shapes(plan):
    rows = (plan.rows, plan.width)
    return [shape(rows, F32)] + [shape(rows, BF16)] * (plan.group - 1)


def summary_scratch(plan):
    return pltpu.VMEM((plan.group * plan.rows, plan.width), F32)


def forward_summary_kernel(plan, rank_ref, codes_ref, k_ref, v_ref, *rest):
    outs, scratch = rest[: plan.group], rest[plan.group]
    cum = running_log(codes_ref[...], 0)
    fall = jnp.exp(cum[plan.tok - 1 : plan.tok, :] - cum)

    def cols(h):
        return slice(h * plan.width, (h + 1) * plan.width)

    def left(h):
        return (fall[:, h : h + 1] * k_ref[:, cols(h)].astype(F32)).astype(BF16)

    put_summaries(plan, rank_ref[0], left, lambda h: v_ref[:, cols(h)], cum, outs, scratch)


def combine_kernel(plan, rank_ref, *rest):
    group, width = plan.group, plan.width
    ins, (pre_ref, total_ref, scratch) = rest[:group], rest[group:]
    rank = rank_ref[0]
    for j in range(group):
        scratch[aligned(rank ^ j, plan.rows), :] = ins[j][...].astype(F32)
    decays = []
    for i in range(plan.quarter):
        held = jnp.zeros((width, width), F32)
        decay = jnp.ones((1, width), F32)
        per_member = []
        for m in range(group):
            base = m * plan.rows
            at = slice(base + i * width, base + (i + 1) * width)
            pre_ref[at, :] = held
            per_member.append(decay)
            total = read_tail(plan, scratch, base, i)
            held = total * held + scratch[at, :]
            decay = decay * total
        decays.append(per_member + [decay])
        total_ref[i * width : (i + 1) * width, :] = held.astype(BF16)
    for m in range(group):
        base = m * plan.rows + plan.body
        pre_ref[base : base + plan.tail, :] = tail_rows(plan, [d[m] for d in decays])
    total_ref[plan.body : plan.rows, :] = tail_rows(plan, [d[group] for d in decays]).astype(BF16)


def spread_kernel(plan, rank_ref, enters_ref, entry_ref, pre_ref, *rest):
    group, width = plan.group, plan.width
    outs, scratch = rest[:group], rest[group]
    rank = rank_ref[0]
    enters = enters_ref[0] > 0
    for i in range(plan.quarter):
        at = slice(i * width, (i + 1) * width)
        entry = jnp.where(enters, entry_ref[at, :].astype(F32), 0.0)
        for m in range(group):
            base = m * plan.rows
            state = read_tail(plan, pre_ref, base, i) * entry
            state = state + pre_ref[base + i * width : base + (i + 1) * width, :]
            to = m * plan.body + i * width
            scratch[to : to + width, :] = state.astype(BF16)
    for j in range(group):
        outs[j][...] = scratch[aligned(rank ^ j, plan.body), :]


def swap(value, axis, offset):
    count = lax.axis_size(axis)
    return lax.ppermute(value, axis, [(i, i ^ offset) for i in range(count)])


def join(plan, earlier, later):
    earlier, later = earlier.astype(F32), later.astype(F32)
    bodies, totals = [], []
    for i in range(plan.quarter):
        at = slice(i * plan.width, (i + 1) * plan.width)
        mine = read_tail(plan, later, 0, i)
        bodies.append(mine * earlier[at] + later[at])
        totals.append(mine * read_tail(plan, earlier, 0, i))
    return jnp.concatenate(bodies + [tail_rows(plan, totals)]).astype(BF16)


def group_entry(plan, total, way, turn):
    count, span = plan.seq, plan.group

    def shift(value, by):
        hop = way * by * span
        return lax.ppermute(value, "seq", [(i, (i + hop) % count) for i in range(count)])

    entry = shift(total, 1)
    by = 1
    while by < plan.groups - 1:
        entry = jnp.where(turn > by, join(plan, shift(entry, by), entry), entry)
        by *= 2
    return entry


def scan_states(plan, summaries, way):
    place = lax.axis_index("seq")
    turn = place if way > 0 else plan.seq - 1 - place
    rank = (turn % plan.group).reshape(1)
    turn = turn // plan.group
    got = [summaries[0]] + [swap(summaries[j], "seq", j) for j in range(1, plan.group)]
    rows, body = (plan.rows, plan.width), (plan.body, plan.width)
    pre, total = call(
        functools.partial(combine_kernel, plan),
        [shape((plan.group * plan.rows, plan.width), F32), shape(rows, BF16)],
        [SMEM] + [VMEM] * plan.group,
        [rank] + got,
        [pltpu.VMEM((plan.group * plan.rows, plan.width), F32)],
    )
    entry = group_entry(plan, total, way, turn)
    states = call(
        functools.partial(spread_kernel, plan),
        [shape(body, BF16)] * plan.group,
        [SMEM, SMEM, VMEM, VMEM],
        [rank, (turn > 0).astype(jnp.int32).reshape(1), entry, pre],
        [pltpu.VMEM((plan.group * plan.body, plan.width), BF16)],
    )
    return [states[0]] + [swap(states[j], "seq", j) for j in range(1, plan.group)]


def gather_states(plan, rank, ins, scratch):
    for j in range(plan.group):
        scratch[aligned(rank ^ j, plan.body), :] = ins[j][...]


def mask_of(plan, cum, cum_t, h):
    size = (plan.tok, plan.tok)
    lower = lax.broadcasted_iota(jnp.int32, size, 0) >= lax.broadcasted_iota(jnp.int32, size, 1)
    gap = cum[:, h : h + 1] - cum_t[h : h + 1, :]
    return jnp.where(lower, jnp.exp(jnp.where(lower, gap, 0.0)), 0.0)


def forward_local_kernel(plan, codes_ref, codes_t_ref, q_ref, k_ref, v_ref, attn_ref, out_ref, rise_ref):
    scale = 1.0 / plan.width
    cum, cum_t = running_log(codes_ref[...], 0), running_log(codes_t_ref[...], 1)
    rise = scale * jnp.exp(cum)
    for h in range(plan.heads):
        at = slice(h * plan.width, (h + 1) * plan.width)
        rows = slice(h * plan.tok, (h + 1) * plan.tok)
        q = q_ref[:, at]
        scores = dot(q, k_ref[:, at], 1, 1)
        attn = (scale * scores * mask_of(plan, cum, cum_t, h)).astype(BF16)
        attn_ref[rows, :] = attn
        out_ref[:, at] = dot(attn, v_ref[:, at], 1, 0)
        rise_ref[:, at] = (rise[:, h : h + 1] * q.astype(F32)).astype(BF16)


def weight_copies(index_ref, weight_ref, buffers, sems, count, width):
    copies = []
    for s in range(count):
        at = pl.ds(pl.multiple_of(index_ref[s] * width, 128), width)
        copies.append(pltpu.make_async_copy(weight_ref.at[:, at], buffers.at[s], sems.at[s]))
        copies[-1].start()
    return copies


def grad_kernel(plan, count, last, rank_ref, index_ref, weight_ref, *rest):
    shards, rest = rest[:count], rest[count:]
    if last:
        before_ref, codes_ref, q_ref, grad_ref = rest[:4]
        outs = rest[4 : 4 + plan.group]
        scratch, buffers, sems = rest[4 + plan.group :]
    else:
        (sum_ref, buffers, sems), before_ref = rest, None
    width = shards[0].shape[1]
    copies = weight_copies(index_ref, weight_ref, buffers, sems, count, width)
    total = None if before_ref is None else before_ref[...]
    for s in range(count):
        copies[s].wait()
        part = dot(shards[s][...], buffers[s], 1, 1)
        total = part if total is None else total + part
    if not last:
        sum_ref[...] = total
        return
    grad_ref[...] = total.astype(BF16)
    cum = running_log(codes_ref[...], 0)
    rise = (1.0 / plan.width) * jnp.exp(cum)

    def cols(h):
        return slice(h * plan.width, (h + 1) * plan.width)

    def left(h):
        return (rise[:, h : h + 1] * q_ref[:, cols(h)].astype(F32)).astype(BF16)

    put_summaries(plan, rank_ref[0], left, lambda h: grad_ref[:, cols(h)], cum, outs, scratch)


def backward_local_kernel(
    plan, codes_ref, codes_t_ref, q_ref, k_ref, v_ref, grad_ref, attn_ref, lq_ref, lk_ref, lv_ref
):
    scale = 1.0 / plan.width
    cum, cum_t = running_log(codes_ref[...], 0), running_log(codes_t_ref[...], 1)
    for h in range(plan.heads):
        at = slice(h * plan.width, (h + 1) * plan.width)
        rows = slice(h * plan.tok, (h + 1) * plan.tok)
        grad = grad_ref[:, at]
        scores = dot(grad, v_ref[:, at], 1, 1)
        pmat = (scale * scores * mask_of(plan, cum, cum_t, h)).astype(BF16)
        lq_ref[:, at] = dot(pmat, k_ref[:, at], 1, 0)
        lk_ref[:, at] = dot(pmat, q_ref[:, at], 0, 0)
        lv_ref[:, at] = dot(attn_ref[rows, :], grad, 0, 0)


def mix_first_kernel(plan, count, rank_ref, index_ref, weight_ref, local_ref, rise_ref, *rest):
    ins, rest = rest[: plan.group], rest[plan.group :]
    flat_ref, outs = rest[0], rest[1 : 1 + count]
    states, buffers, sems = rest[1 + count :]
    copies = weight_copies(index_ref, weight_ref, buffers, sems, count, outs[0].shape[1])
    gather_states(plan, rank_ref[0], ins, states)
    for h in range(plan.heads):
        at = slice(h * plan.width, (h + 1) * plan.width)
        cross = dot(rise_ref[:, at], states[at, :], 1, 0)
        flat_ref[:, at] = (local_ref[:, at] + cross).astype(BF16)
    for s in range(count):
        copies[s].wait()
        outs[s][...] = dot(flat_ref[...], buffers[s], 1, 0).astype(outs[s].dtype)


def mix_second_kernel(plan, count, index_ref, weight_ref, flat_ref, *rest):
    outs, (buffers, sems) = rest[:count], rest[count:]
    copies = weight_copies(index_ref, weight_ref, buffers, sems, count, outs[0].shape[1])
    for s in range(count):
        copies[s].wait()
        outs[s][...] = dot(flat_ref[...], buffers[s], 1, 0).astype(outs[s].dtype)


def query_grad_kernel(plan, rank_ref, codes_ref, local_ref, grad_ref, *rest):
    ins, (out_ref, states) = rest[: plan.group], rest[plan.group :]
    gather_states(plan, rank_ref[0], ins, states)
    rise = (1.0 / plan.width) * jnp.exp(running_log(codes_ref[...], 0))
    for h in range(plan.heads):
        at = slice(h * plan.width, (h + 1) * plan.width)
        g_rise = (rise[:, h : h + 1] * grad_ref[:, at].astype(F32)).astype(BF16)
        out_ref[:, at] = (local_ref[:, at] + dot(g_rise, states[at, :], 1, 1)).astype(BF16)


def key_value_grad_kernel(plan, rank_ref, codes_ref, k_ref, v_ref, lk_ref, lv_ref, *rest):
    ins, (kg_ref, vg_ref, states) = rest[: plan.group], rest[plan.group :]
    gather_states(plan, rank_ref[0], ins, states)
    cum = running_log(codes_ref[...], 0)
    fall = jnp.exp(cum[plan.tok - 1 : plan.tok, :] - cum)
    for h in range(plan.heads):
        at = slice(h * plan.width, (h + 1) * plan.width)
        carry = states[at, :]
        v_fall = (fall[:, h : h + 1] * v_ref[:, at].astype(F32)).astype(BF16)
        k_fall = (fall[:, h : h + 1] * k_ref[:, at].astype(F32)).astype(BF16)
        kg_ref[:, at] = (lk_ref[:, at] + dot(v_fall, carry, 1, 1)).astype(BF16)
        vg_ref[:, at] = (lv_ref[:, at] + dot(k_fall, carry, 1, 0)).astype(BF16)


def local(queries, keys, values, decay_codes, out_weight, out_grad):
    tok, flat = queries.shape
    heads = decay_codes.shape[1]
    plan = Plan(tok, heads, flat // heads, lax.axis_size("seq"))
    across, feat = lax.axis_size("head"), out_grad.shape[1]
    place, mine = lax.axis_index("seq"), lax.axis_index("head")
    rank = (place % plan.group).reshape(1)
    rank_back = ((plan.seq - 1 - place) % plan.group).reshape(1)
    codes_t = decay_codes.T
    deep = out_weight.shape[0]

    def order(offsets):
        return jnp.stack([mine ^ o for o in offsets]).astype(jnp.int32)

    def buffers(count):
        return [pltpu.VMEM((count, deep, feat), BF16), pltpu.SemaphoreType.DMA((count,))]

    shards = {0: out_grad}
    hop = across // 2
    while hop:
        shards.update({o ^ hop: swap(part, "head", hop) for o, part in list(shards.items())})
        hop //= 2
    half = across // 2

    summaries = call(
        functools.partial(forward_summary_kernel, plan),
        summary_shapes(plan),
        [SMEM, VMEM, VMEM, VMEM],
        [rank, decay_codes, keys, values],
        [summary_scratch(plan)],
        flops=2 * tok * flat * plan.width,
        nbytes=4 * tok * flat,
    )
    states = scan_states(plan, summaries, 1)

    wide = (tok, flat)
    near, far = list(range(half)), list(range(half, across))
    (part,) = call(
        functools.partial(grad_kernel, plan, half, False),
        [shape(wide, F32)],
        [SMEM, SMEM, HBM] + [VMEM] * half,
        [rank, order(near), out_weight] + [shards[o] for o in near],
        buffers(half),
        flops=2 * tok * flat * feat * half,
        nbytes=2 * flat * feat * half,
    )
    grad, *summaries_back = call(
        functools.partial(grad_kernel, plan, half, True),
        [shape(wide, BF16)] + summary_shapes(plan),
        [SMEM, SMEM, HBM] + [VMEM] * (half + 3),
        [rank_back, order(far), out_weight] + [shards[o] for o in far] + [part, decay_codes, queries],
        [summary_scratch(plan)] + buffers(half),
        flops=2 * tok * flat * feat * half,
        nbytes=2 * flat * feat * half,
    )
    carries = scan_states(plan, summaries_back, -1)

    attn, local_out, q_rise = call(
        functools.partial(forward_local_kernel, plan),
        [shape((heads * tok, tok), BF16), shape(wide, F32), shape(wide, BF16)],
        [VMEM] * 5,
        [decay_codes, codes_t, queries, keys, values],
        flops=4 * tok * flat * plan.width,
        nbytes=14 * tok * flat,
    )
    local_q, local_k, local_v = call(
        functools.partial(backward_local_kernel, plan),
        [shape(wide, F32)] * 3,
        [VMEM] * 7,
        [decay_codes, codes_t, queries, keys, values, grad, attn],
        flops=8 * tok * flat * plan.width,
        nbytes=22 * tok * flat,
    )

    held = pltpu.VMEM((flat, plan.width), BF16)
    far = far[::-1]
    attn_out, *sent = call(
        functools.partial(mix_first_kernel, plan, half),
        [shape(wide, BF16)] + [shape((tok, feat), BF16)] * half,
        [SMEM, SMEM, HBM, VMEM, VMEM] + [VMEM] * plan.group,
        [rank, order(far), out_weight, local_out, q_rise] + states,
        [held] + buffers(half),
        flops=2 * tok * flat * feat * half,
        nbytes=2 * flat * feat * half,
    )
    near = near[::-1]
    kept = call(
        functools.partial(mix_second_kernel, plan, half),
        [shape((tok, feat), F32 if o == 0 else BF16) for o in near],
        [SMEM, HBM, VMEM],
        [order(near), out_weight, attn_out],
        buffers(half),
        flops=2 * tok * flat * feat * half,
        nbytes=2 * flat * feat * half,
    )

    def halve(parts, hop):
        moved = {o: swap(part, "head", hop) for o, part in parts.items() if o & hop}
        return {
            o: (part.astype(F32) + moved[o | hop].astype(F32)).astype(F32 if o == 0 else BF16)
            for o, part in parts.items()
            if not o & hop
        }

    far_parts, near_parts = dict(zip(far, sent)), dict(zip(near, kept))
    hop = 1
    while hop < half:
        far_parts, near_parts = halve(far_parts, hop), halve(near_parts, hop)
        hop *= 2
    mixed = halve({**far_parts, **near_parts}, half)[0].astype(BF16)

    (query_grad,) = call(
        functools.partial(query_grad_kernel, plan),
        [shape(wide, BF16)],
        [SMEM] + [VMEM] * (3 + plan.group),
        [rank, decay_codes, local_q, grad] + states,
        [held],
        flops=2 * tok * flat * plan.width,
        nbytes=10 * tok * flat,
    )
    key_grad, value_grad = call(
        functools.partial(key_value_grad_kernel, plan),
        [shape(wide, BF16)] * 2,
        [SMEM] + [VMEM] * (5 + plan.group),
        [rank_back, decay_codes, keys, values, local_k, local_v] + carries,
        [held],
        flops=4 * tok * flat * plan.width,
        nbytes=18 * tok * flat,
    )
    return mixed, query_grad, key_grad, value_grad


def solution(mesh):
    whole = P("seq", "head")
    return jax.shard_map(
        local,
        mesh=mesh,
        in_specs=(whole, whole, whole, whole, P("head", None), whole),
        out_specs=(whole,) * 4,
        check_vma=False,
    )
```

```python
import functools

import jax
import jax.numpy as jnp
from jax import lax
from jax.experimental import pallas as pl
from jax.experimental.pallas import tpu as pltpu
from jax.sharding import PartitionSpec as P


F32 = jnp.float32
BF16 = jnp.bfloat16
VMEM = pl.BlockSpec(memory_space=pltpu.VMEM)
SMEM = pl.BlockSpec(memory_space=pltpu.SMEM)
HBM = pl.BlockSpec(memory_space=pltpu.HBM)


def dot(a, b, ca, cb):
    return lax.dot_general(a, b, (((ca,), (cb,)), ((), ())), preferred_element_type=F32)


def aligned(index, size):
    return pl.ds(pl.multiple_of(index * size, size), size)


def call(kernel, outs, specs, args, scratch=(), limit=16, flops=0, nbytes=0):
    return pl.pallas_call(
        kernel,
        out_shape=outs,
        in_specs=specs,
        out_specs=[VMEM] * len(outs),
        scratch_shapes=list(scratch),
        compiler_params=pltpu.CompilerParams(vmem_limit_bytes=limit << 20),
        cost_estimate=pl.CostEstimate(flops=flops, bytes_accessed=nbytes, transcendentals=0),
    )(*args)


def in_hbm(array):
    return pltpu.with_memory_space_constraint(array, pltpu.HBM)


def shape(dims, dtype):
    return jax.ShapeDtypeStruct(dims, dtype)


def running_log(codes_ref):
    total = jnp.log(1.0 - codes_ref[...].astype(F32) / 4096.0)
    place = lax.broadcasted_iota(jnp.int32, total.shape, 1)
    step = 1
    while step < total.shape[1]:
        total = total + jnp.where(place >= step, pltpu.roll(total, step, 1), 0.0)
        step *= 2
    return total


def running_pair(codes_ref):
    cum_t = running_log(codes_ref)
    return cum_t.T, cum_t


def positions(plan, way):
    place = lax.axis_index("seq")
    turn = place if way > 0 else plan.seq - 1 - place
    return lax.rem(turn, plan.group), lax.div(turn, plan.group)


class Plan:
    def __init__(self, tok, heads, width, seq):
        self.tok, self.heads, self.width, self.seq = tok, heads, width, seq
        self.group = next(g for g in (4, 2, 1) if heads % g == 0 and seq % g == 0)
        self.groups = seq // self.group
        self.quarter = heads // self.group
        self.half_tail = 8 * pl.cdiv(self.quarter, 8)
        self.tail = 2 * self.half_tail
        self.body = self.quarter * width
        self.rows = self.body + self.tail


def tail_rows(plan, totals):
    place = lax.broadcasted_iota(jnp.int32, (plan.tail, plan.width), 0)
    rows = jnp.zeros((plan.tail, plan.width), F32)
    for i, total in enumerate(totals):
        high = total.astype(BF16).astype(F32)
        rows = jnp.where(place == i, high, rows)
        rows = jnp.where(place == plan.half_tail + i, total - high, rows)
    return rows


def read_tail(plan, ref, base, i):
    at = base + plan.body + i
    return ref[at : at + 1, :] + ref[at + plan.half_tail : at + plan.half_tail + 1, :]


def put_summaries(plan, rank, left, right, cum, outs, scratch, arrive=None):
    width = plan.width
    last = jnp.exp(cum[plan.tok - 1 : plan.tok, :])
    for q in range(plan.group):
        base = q * plan.rows
        totals = []
        if arrive is not None:
            arrive(q)
        for i in range(plan.quarter):
            h = q * plan.quarter + i
            scratch[base + i * width : base + (i + 1) * width, :] = dot(left(h), right(h), 0, 0)
            totals.append(jnp.broadcast_to(last[:, h : h + 1], (1, width)))
        scratch[base + plan.body : base + plan.rows, :] = tail_rows(plan, totals)
    outs[0][...] = scratch[aligned(rank, plan.rows), :]
    for j in range(1, plan.group):
        outs[j][...] = scratch[aligned(rank ^ j, plan.rows), :].astype(BF16)


def summary_shapes(plan):
    rows = (plan.rows, plan.width)
    return [shape(rows, F32)] + [shape(rows, BF16)] * (plan.group - 1)


def summary_scratch(plan):
    return pltpu.VMEM((plan.group * plan.rows, plan.width), F32)


def forward_summary_kernel(plan, *refs):
    codes, keys, values, queries = refs[:4]
    outs, rest = refs[4 : 4 + plan.group], refs[4 + plan.group :]
    codes_ref, k_ref, v_ref, q_ref, scratch, sems = rest
    wide = plan.quarter * plan.width
    loads = [pltpu.make_async_copy(codes, codes_ref, sems.at[0])]
    for q in range(plan.group):
        at = slice(q * wide, (q + 1) * wide)
        loads.append(pltpu.make_async_copy(keys.at[:, at], k_ref.at[:, at], sems.at[2 * q + 1]))
        loads.append(pltpu.make_async_copy(values.at[:, at], v_ref.at[:, at], sems.at[2 * q + 2]))
    loads.append(pltpu.make_async_copy(queries, q_ref, sems.at[2 * plan.group + 1]))
    for load in loads:
        load.start()
    loads[0].wait()
    cum, _ = running_pair(codes_ref)
    fall = jnp.exp(cum[plan.tok - 1 : plan.tok, :] - cum)

    def cols(h):
        return slice(h * plan.width, (h + 1) * plan.width)

    def arrive(q):
        loads[2 * q + 1].wait()
        loads[2 * q + 2].wait()

    def left(h):
        return (fall[:, h : h + 1] * k_ref[:, cols(h)].astype(F32)).astype(BF16)

    rank = positions(plan, 1)[0]
    put_summaries(plan, rank, left, lambda h: v_ref[:, cols(h)], cum, outs, scratch, arrive)
    loads[-1].wait()


def combine_kernel(plan, way, *rest):
    group, width = plan.group, plan.width
    ins, (pre_ref, total_ref, scratch) = rest[:group], rest[group:]
    rank = positions(plan, way)[0]
    for j in range(group):
        scratch[aligned(rank ^ j, plan.rows), :] = ins[j][...].astype(F32)
    decays = []
    for i in range(plan.quarter):
        held = jnp.zeros((width, width), F32)
        decay = jnp.ones((1, width), F32)
        per_member = []
        for m in range(group):
            base = m * plan.rows
            at = slice(base + i * width, base + (i + 1) * width)
            pre_ref[at, :] = held
            per_member.append(decay)
            total = read_tail(plan, scratch, base, i)
            held = total * held + scratch[at, :]
            decay = decay * total
        decays.append(per_member + [decay])
        total_ref[i * width : (i + 1) * width, :] = held.astype(BF16)
    for m in range(group):
        base = m * plan.rows + plan.body
        pre_ref[base : base + plan.tail, :] = tail_rows(plan, [d[m] for d in decays])
    total_ref[plan.body : plan.rows, :] = tail_rows(plan, [d[group] for d in decays]).astype(BF16)


def spread_kernel(plan, way, entry_ref, pre_ref, *rest):
    group, width = plan.group, plan.width
    outs, scratch = rest[:group], rest[group]
    rank, turn = positions(plan, way)
    enters = turn > 0
    for i in range(plan.quarter):
        at = slice(i * width, (i + 1) * width)
        entry = jnp.where(enters, entry_ref[at, :].astype(F32), 0.0)
        for m in range(group):
            base = m * plan.rows
            state = read_tail(plan, pre_ref, base, i) * entry
            state = state + pre_ref[base + i * width : base + (i + 1) * width, :]
            to = m * plan.body + i * width
            scratch[to : to + width, :] = state.astype(BF16)
    for j in range(group):
        outs[j][...] = scratch[aligned(rank ^ j, plan.body), :]


def swap(value, axis, offset):
    count = lax.axis_size(axis)
    return lax.ppermute(value, axis, [(i, i ^ offset) for i in range(count)])


def join(plan, earlier, later):
    earlier, later = earlier.astype(F32), later.astype(F32)
    bodies, totals = [], []
    for i in range(plan.quarter):
        at = slice(i * plan.width, (i + 1) * plan.width)
        mine = read_tail(plan, later, 0, i)
        bodies.append(mine * earlier[at] + later[at])
        totals.append(mine * read_tail(plan, earlier, 0, i))
    return jnp.concatenate(bodies + [tail_rows(plan, totals)]).astype(BF16)


def group_entry(plan, total, way, turn):
    count, span = plan.seq, plan.group

    def shift(value, by):
        hop = way * by * span
        return lax.ppermute(value, "seq", [(i, (i + hop) % count) for i in range(count)])

    entry = shift(total, 1)
    by = 1
    while by < plan.groups - 1:
        entry = jnp.where(turn > by, join(plan, shift(entry, by), entry), entry)
        by *= 2
    return entry


def scan_states(plan, summaries, way):
    turn = positions(plan, way)[1]
    others = range(1, plan.group)
    got = [summaries[0]] + [swap(summaries[j], "seq", j) for j in others]
    rows, body = (plan.rows, plan.width), (plan.body, plan.width)
    pre, total = call(
        functools.partial(combine_kernel, plan, way),
        [shape((plan.group * plan.rows, plan.width), F32), shape(rows, BF16)],
        [VMEM] * plan.group,
        got,
        [pltpu.VMEM((plan.group * plan.rows, plan.width), F32)],
    )
    entry = group_entry(plan, total, way, turn)
    states = call(
        functools.partial(spread_kernel, plan, way),
        [shape(body, BF16)] * plan.group,
        [VMEM, VMEM],
        [entry, pre],
        [pltpu.VMEM((plan.group * plan.body, plan.width), BF16)],
    )
    return [states[0]] + [swap(states[j], "seq", j) for j in others]


def gather_states(plan, way, ins, scratch):
    rank = positions(plan, way)[0]
    for j in range(plan.group):
        scratch[aligned(rank ^ j, plan.body), :] = ins[j][...]


def mask_of(plan, cum, cum_t, h):
    size = (plan.tok, plan.tok)
    lower = lax.broadcasted_iota(jnp.int32, size, 0) >= lax.broadcasted_iota(jnp.int32, size, 1)
    gap = cum[:, h : h + 1] - cum_t[h : h + 1, :]
    return jnp.where(lower, jnp.exp(jnp.where(lower, gap, 0.0)), 0.0)


def forward_local_kernel(plan, codes_ref, q_ref, k_ref, v_ref, attn_ref, out_ref, rise_ref):
    scale = 1.0 / plan.width
    cum, cum_t = running_pair(codes_ref)
    rise = scale * jnp.exp(cum)
    for h in range(plan.heads):
        at = slice(h * plan.width, (h + 1) * plan.width)
        rows = slice(h * plan.tok, (h + 1) * plan.tok)
        q = q_ref[:, at]
        scores = dot(q, k_ref[:, at], 1, 1)
        attn = (scale * scores * mask_of(plan, cum, cum_t, h)).astype(BF16)
        attn_ref[rows, :] = attn
        out_ref[:, at] = dot(attn, v_ref[:, at], 1, 0)
        rise_ref[:, at] = (rise[:, h : h + 1] * q.astype(F32)).astype(BF16)


def weight_columns(offset, width):
    return aligned(lax.axis_index("head") ^ offset, width)


def near_grad_kernel(near, far, weight, first, *rest):
    shards, (sum_ref, weight_ref, first_ref, sems, first_sem) = rest[:-5], rest[-5:]
    width, rows = first.shape[1], weight.shape[0] // 2
    load_first = pltpu.make_async_copy(first, first_ref, first_sem)
    load_first.start()
    loads = []
    for offset in near + far:
        columns = weight_columns(offset, width)
        for part in range(2):
            at = (slice(part * rows, (part + 1) * rows), columns)
            sem = sems.at[len(loads)]
            loads.append(pltpu.make_async_copy(weight.at[at], weight_ref.at[at], sem))
    ahead = 2 * len(near)
    for load in loads[:ahead]:
        load.start()
    load_first.wait()
    for i, offset in enumerate(near):
        shard = (first_ref if i == 0 else shards[i - 1])[...]
        columns = weight_columns(offset, width)
        for part in range(2):
            at = slice(part * rows, (part + 1) * rows)
            loads[2 * i + part].wait()
            loads[ahead + 2 * i + part].start()
            product = dot(shard, weight_ref[at, columns], 1, 1)
            sum_ref[:, at] = product if i == 0 else sum_ref[:, at] + product
    for load in loads[ahead:]:
        load.wait()


def far_grad_kernel(plan, offsets, weight_ref, *rest):
    count = len(offsets)
    shards, (before_ref, codes_ref, q_ref, grad_ref) = rest[:count], rest[count : count + 4]
    outs, scratch = rest[count + 4 : -1], rest[-1]
    width = shards[0].shape[1]
    total = before_ref[...]
    for offset, shard in zip(offsets, shards):
        total = total + dot(shard[...], weight_ref[:, weight_columns(offset, width)], 1, 1)
    grad_ref[...] = total.astype(BF16)
    cum, _ = running_pair(codes_ref)
    rise = (1.0 / plan.width) * jnp.exp(cum)

    def cols(h):
        return slice(h * plan.width, (h + 1) * plan.width)

    def left(h):
        return (rise[:, h : h + 1] * q_ref[:, cols(h)].astype(F32)).astype(BF16)

    put_summaries(plan, positions(plan, -1)[0], left, lambda h: grad_ref[:, cols(h)], cum, outs, scratch)


def backward_local_kernel(
    plan, codes_ref, q_ref, k_ref, v_ref, grad_ref, attn_ref, lq_ref, lk_ref, lv_ref
):
    scale = 1.0 / plan.width
    cum, cum_t = running_pair(codes_ref)
    for h in range(plan.heads):
        at = slice(h * plan.width, (h + 1) * plan.width)
        rows = slice(h * plan.tok, (h + 1) * plan.tok)
        grad = grad_ref[:, at]
        scores = dot(grad, v_ref[:, at], 1, 1)
        pmat = (scale * scores * mask_of(plan, cum, cum_t, h)).astype(BF16)
        lq_ref[:, at] = dot(pmat, k_ref[:, at], 1, 0)
        lk_ref[:, at] = dot(pmat, q_ref[:, at], 0, 0)
        lv_ref[:, at] = dot(attn_ref[rows, :], grad, 0, 0)


def mix(offsets, weight_ref, flat_ref, outs):
    for offset, out in zip(offsets, outs):
        columns = weight_ref[:, weight_columns(offset, out.shape[1])]
        out[...] = dot(flat_ref[...], columns, 1, 0).astype(out.dtype)


def mix_first_kernel(plan, offsets, weight_ref, local_ref, rise_ref, *rest):
    ins, (flat_ref, *outs, states) = rest[: plan.group], rest[plan.group :]
    gather_states(plan, 1, ins, states)
    for h in range(plan.heads):
        at = slice(h * plan.width, (h + 1) * plan.width)
        cross = dot(rise_ref[:, at], states[at, :], 1, 0)
        flat_ref[:, at] = (local_ref[:, at] + cross).astype(BF16)
    mix(offsets, weight_ref, flat_ref, outs)


def mix_second_kernel(offsets, weight_ref, flat_ref, *outs):
    mix(offsets, weight_ref, flat_ref, outs)


def query_grad_kernel(plan, codes_ref, local_ref, grad_ref, *rest):
    ins, (out_ref, states) = rest[: plan.group], rest[plan.group :]
    gather_states(plan, 1, ins, states)
    rise = (1.0 / plan.width) * jnp.exp(running_pair(codes_ref)[0])
    for h in range(plan.heads):
        at = slice(h * plan.width, (h + 1) * plan.width)
        g_rise = (rise[:, h : h + 1] * grad_ref[:, at].astype(F32)).astype(BF16)
        out_ref[:, at] = (local_ref[:, at] + dot(g_rise, states[at, :], 1, 1)).astype(BF16)


def key_value_grad_kernel(plan, codes_ref, k_ref, v_ref, lk_ref, lv_ref, *rest):
    ins, (kg_ref, vg_ref, states) = rest[: plan.group], rest[plan.group :]
    gather_states(plan, -1, ins, states)
    cum, _ = running_pair(codes_ref)
    fall = jnp.exp(cum[plan.tok - 1 : plan.tok, :] - cum)
    for h in range(plan.heads):
        at = slice(h * plan.width, (h + 1) * plan.width)
        carry = states[at, :]
        v_fall = (fall[:, h : h + 1] * v_ref[:, at].astype(F32)).astype(BF16)
        k_fall = (fall[:, h : h + 1] * k_ref[:, at].astype(F32)).astype(BF16)
        kg_ref[:, at] = (lk_ref[:, at] + dot(v_fall, carry, 1, 1)).astype(BF16)
        vg_ref[:, at] = (lv_ref[:, at] + dot(k_fall, carry, 1, 0)).astype(BF16)


def local(queries, keys, values, decay_codes, out_weight, out_grad):
    tok, flat = queries.shape
    heads = decay_codes.shape[1]
    plan = Plan(tok, heads, flat // heads, lax.axis_size("seq"))
    across, feat = lax.axis_size("head"), out_grad.shape[1]
    codes = decay_codes.T
    half = across // 2
    wide = (tok, flat)
    near, far = list(range(half)), list(range(half, across))

    shards = {0: out_grad}
    hop = half
    while hop:
        for o, part in list(shards.items()):
            shards[o ^ hop] = swap(part, "head", hop)
        hop //= 2

    *summaries, codes, keys, values, queries = call(
        functools.partial(forward_summary_kernel, plan),
        summary_shapes(plan) + [shape(x.shape, x.dtype) for x in (codes, keys, values, queries)],
        [HBM] * 4,
        [in_hbm(x) for x in (codes, keys, values, queries)],
        [summary_scratch(plan), pltpu.SemaphoreType.DMA((2 * plan.group + 2,))],
        flops=2 * tok * flat * plan.width,
        nbytes=4 * tok * flat,
    )
    states = scan_states(plan, summaries, 1)

    matmul = dict(flops=2 * tok * flat * feat * half, nbytes=2 * flat * feat * half)
    part, out_weight = call(
        functools.partial(near_grad_kernel, near, far),
        [shape(wide, F32), shape(out_weight.shape, BF16)],
        [HBM] * 2 + [VMEM] * (half - 1),
        [in_hbm(out_weight), in_hbm(out_grad)] + [shards[o] for o in near[1:]],
        [
            pltpu.VMEM(out_grad.shape, BF16),
            pltpu.SemaphoreType.DMA((2 * across,)),
            pltpu.SemaphoreType.DMA,
        ],
        **matmul,
    )
    grad, *summaries_back = call(
        functools.partial(far_grad_kernel, plan, far),
        [shape(wide, BF16)] + summary_shapes(plan),
        [VMEM] * (half + 4),
        [out_weight] + [shards[o] for o in far] + [part, codes, queries],
        [summary_scratch(plan)],
        **matmul,
    )
    carries = scan_states(plan, summaries_back, -1)

    attn, local_out, q_rise = call(
        functools.partial(forward_local_kernel, plan),
        [shape((heads * tok, tok), BF16), shape(wide, F32), shape(wide, BF16)],
        [VMEM] * 4,
        [codes, queries, keys, values],
        flops=4 * tok * flat * plan.width,
        nbytes=14 * tok * flat,
    )
    local_q, local_k, local_v = call(
        functools.partial(backward_local_kernel, plan),
        [shape(wide, F32)] * 3,
        [VMEM] * 6,
        [codes, queries, keys, values, grad, attn],
        flops=8 * tok * flat * plan.width,
        nbytes=22 * tok * flat,
    )

    held = pltpu.VMEM((flat, plan.width), BF16)
    far, near = far[::-1], near[::-1]
    attn_out, *sent = call(
        functools.partial(mix_first_kernel, plan, far),
        [shape(wide, BF16)] + [shape((tok, feat), BF16)] * half,
        [VMEM] * (3 + plan.group),
        [out_weight, local_out, q_rise] + states,
        [held],
        **matmul,
    )
    kept = call(
        functools.partial(mix_second_kernel, near),
        [shape((tok, feat), F32 if o == 0 else BF16) for o in near],
        [VMEM] * 2,
        [out_weight, attn_out],
        **matmul,
    )

    def halve(parts, hop):
        moved = {o: swap(part, "head", hop) for o, part in parts.items() if o & hop}
        return {
            o: (part.astype(F32) + moved[o | hop].astype(F32)).astype(F32 if o == 0 else BF16)
            for o, part in parts.items()
            if not o & hop
        }

    far_parts, near_parts = dict(zip(far, sent)), dict(zip(near, kept))
    hop = 1
    while hop < half:
        far_parts, near_parts = halve(far_parts, hop), halve(near_parts, hop)
        hop *= 2
    mixed = halve({**far_parts, **near_parts}, half)[0].astype(BF16)

    (query_grad,) = call(
        functools.partial(query_grad_kernel, plan),
        [shape(wide, BF16)],
        [VMEM] * (3 + plan.group),
        [codes, local_q, grad] + states,
        [held],
        flops=2 * tok * flat * plan.width,
        nbytes=10 * tok * flat,
    )
    key_grad, value_grad = call(
        functools.partial(key_value_grad_kernel, plan),
        [shape(wide, BF16)] * 2,
        [VMEM] * (5 + plan.group),
        [codes, keys, values, local_k, local_v] + carries,
        [held],
        flops=4 * tok * flat * plan.width,
        nbytes=18 * tok * flat,
    )
    return mixed, query_grad, key_grad, value_grad


def solution(mesh):
    whole = P("seq", "head")

    return jax.shard_map(
        local,
        mesh=mesh,
        in_specs=(whole, whole, whole, whole, P("head", None), whole),
        out_specs=(whole,) * 4,
        check_vma=False,
    )
```

```python
import functools

import jax
import jax.numpy as jnp
from jax import lax
from jax.experimental import pallas as pl
from jax.experimental.pallas import tpu as pltpu
from jax.sharding import PartitionSpec as P


F32 = jnp.float32
BF16 = jnp.bfloat16
VMEM = pl.BlockSpec(memory_space=pltpu.VMEM)
SMEM = pl.BlockSpec(memory_space=pltpu.SMEM)
HBM = pl.BlockSpec(memory_space=pltpu.HBM)


def dot(a, b, ca, cb):
    return lax.dot_general(a, b, (((ca,), (cb,)), ((), ())), preferred_element_type=F32)


def aligned(index, size):
    return pl.ds(pl.multiple_of(index * size, size), size)


def call(kernel, outs, specs, args, scratch=(), limit=16, out_specs=None):
    return pl.pallas_call(
        kernel,
        out_shape=outs,
        in_specs=specs,
        out_specs=out_specs or [VMEM] * len(outs),
        scratch_shapes=list(scratch),
        compiler_params=pltpu.CompilerParams(vmem_limit_bytes=limit << 20),
        cost_estimate=pl.CostEstimate(flops=2_400_000_000, bytes_accessed=8_000_000, transcendentals=0),
    )(*args)


def in_hbm(array):
    return pltpu.with_memory_space_constraint(array, pltpu.HBM)


def shape(dims, dtype):
    return jax.ShapeDtypeStruct(dims, dtype)


def running_log(codes):
    rest = jnp.log(1.0 - codes.astype(F32) / 4096.0)
    size = (codes.shape[1], codes.shape[1])
    place, other = (lax.broadcasted_iota(jnp.int32, size, axis) for axis in (0, 1))
    lower = (other <= place).astype(F32).astype(BF16)
    columns = rows = None
    for _ in range(3):
        part = rest.astype(BF16)
        rest = rest - part.astype(F32)
        column, row = dot(lower, part, 1, 1), dot(part, lower, 1, 1)
        columns = column if columns is None else columns + column
        rows = row if rows is None else rows + row
    return columns, rows


def positions(plan, way):
    place = lax.axis_index("seq")
    turn = place if way > 0 else plan.seq - 1 - place
    return lax.rem(turn, plan.group), lax.div(turn, plan.group)


class Plan:
    def __init__(self, tok, heads, width, seq):
        self.tok, self.heads, self.width, self.seq = tok, heads, width, seq
        self.group = next(g for g in (4, 2, 1) if heads % g == 0 and seq % g == 0)
        self.groups = seq // self.group
        self.quarter = heads // self.group
        self.half_tail = 8 * pl.cdiv(self.quarter, 8)
        self.tail = 2 * self.half_tail
        self.body = self.quarter * width
        self.rows = self.body + self.tail


def tail_rows(plan, totals):
    place = lax.broadcasted_iota(jnp.int32, (plan.tail, plan.width), 0)
    rows = jnp.zeros((plan.tail, plan.width), F32)
    for i, total in enumerate(totals):
        high = total.astype(BF16).astype(F32)
        rows = jnp.where(place == i, high, rows)
        rows = jnp.where(place == plan.half_tail + i, total - high, rows)
    return rows


def read_tail(plan, ref, base, i):
    at = base + plan.body + i
    return ref[at : at + 1, :] + ref[at + plan.half_tail : at + plan.half_tail + 1, :]


def put_summaries(plan, rank, left, right, cum, outs, scratch, arrive=None):
    width = plan.width
    last = jnp.exp(cum[plan.tok - 1 : plan.tok, :])
    for q in range(plan.group):
        base = q * plan.rows
        totals = []
        if arrive is not None:
            arrive(q)
        for i in range(plan.quarter):
            h = q * plan.quarter + i
            scratch[base + i * width : base + (i + 1) * width, :] = dot(left(h), right(h), 0, 0)
            totals.append(jnp.broadcast_to(last[:, h : h + 1], (1, width)))
        scratch[base + plan.body : base + plan.rows, :] = tail_rows(plan, totals)
    outs[0][...] = scratch[aligned(rank, plan.rows), :]
    for j in range(1, plan.group):
        outs[j][...] = scratch[aligned(rank ^ j, plan.rows), :].astype(BF16)


def summary_shapes(plan):
    rows = (plan.rows, plan.width)
    return [shape(rows, F32)] + [shape(rows, BF16)] * (plan.group - 1)


def summary_scratch(plan):
    return pltpu.VMEM((plan.group * plan.rows, plan.width), F32)


def first_kernel(plan, codes, keys, values, queries, *refs):
    outs, refs = refs[: plan.group], refs[plan.group :]
    cum_ref, cum_t_ref, rise_ref, fall_ref, k_fall_ref, k_ref, v_ref, q_ref = refs[:8]
    scratch, codes_ref, sems = refs[8:]
    loads = []

    def load(src, dst):
        copy = pltpu.make_async_copy(src, dst, sems.at[len(loads)])
        copy.start()
        loads.append(copy)
        return copy

    wide = plan.quarter * plan.width
    codes_load = load(codes, codes_ref)
    pieces = []
    for q in range(plan.group):
        at = slice(q * wide, (q + 1) * wide)
        pieces.append((load(keys.at[:, at], k_ref.at[:, at]), load(values.at[:, at], v_ref.at[:, at])))
    late = [load(queries, q_ref)]

    codes_load.wait()
    cum, cum_t = running_log(codes_ref[...])
    fall = jnp.exp(cum[plan.tok - 1 : plan.tok, :] - cum)
    cum_ref[...], cum_t_ref[...] = cum, cum_t
    rise_ref[...] = (1.0 / plan.width) * jnp.exp(cum)
    fall_ref[...] = fall

    def cols(h):
        return slice(h * plan.width, (h + 1) * plan.width)

    def arrive(q):
        for piece in pieces[q]:
            piece.wait()

    def left(h):
        k_fall = (fall[:, h : h + 1] * k_ref[:, cols(h)].astype(F32)).astype(BF16)
        k_fall_ref[:, cols(h)] = k_fall
        return k_fall

    rank = positions(plan, 1)[0]
    put_summaries(plan, rank, left, lambda h: v_ref[:, cols(h)], cum, outs, scratch, arrive)
    for copy in late:
        copy.wait()


def combine_kernel(plan, way, *rest):
    group, width = plan.group, plan.width
    ins, (pre_ref, total_ref, scratch) = rest[:group], rest[group:]
    rank = positions(plan, way)[0]
    for j in range(group):
        scratch[aligned(rank ^ j, plan.rows), :] = ins[j][...].astype(F32)
    decays = []
    for i in range(plan.quarter):
        held = jnp.zeros((width, width), F32)
        decay = jnp.ones((1, width), F32)
        per_member = []
        for m in range(group):
            base = m * plan.rows
            at = slice(base + i * width, base + (i + 1) * width)
            pre_ref[at, :] = held
            per_member.append(decay)
            total = read_tail(plan, scratch, base, i)
            held = total * held + scratch[at, :]
            decay = decay * total
        decays.append(per_member + [decay])
        total_ref[i * width : (i + 1) * width, :] = held.astype(BF16)
    for m in range(group):
        base = m * plan.rows + plan.body
        pre_ref[base : base + plan.tail, :] = tail_rows(plan, [d[m] for d in decays])
    total_ref[plan.body : plan.rows, :] = tail_rows(plan, [d[group] for d in decays]).astype(BF16)


def spread_kernel(plan, way, entry_ref, pre_ref, *rest):
    group, width = plan.group, plan.width
    outs, scratch = rest[:group], rest[group]
    rank, turn = positions(plan, way)
    enters = turn > 0
    for i in range(plan.quarter):
        at = slice(i * width, (i + 1) * width)
        entry = jnp.where(enters, entry_ref[at, :].astype(F32), 0.0)
        for m in range(group):
            base = m * plan.rows
            state = read_tail(plan, pre_ref, base, i) * entry
            state = state + pre_ref[base + i * width : base + (i + 1) * width, :]
            to = m * plan.body + i * width
            scratch[to : to + width, :] = state.astype(BF16)
    for j in range(group):
        outs[j][...] = scratch[aligned(rank ^ j, plan.body), :]


def swap(value, axis, offset):
    count = lax.axis_size(axis)
    return lax.ppermute(value, axis, [(i, i ^ offset) for i in range(count)])


def join(plan, earlier, later):
    earlier, later = earlier.astype(F32), later.astype(F32)
    bodies, totals = [], []
    for i in range(plan.quarter):
        at = slice(i * plan.width, (i + 1) * plan.width)
        mine = read_tail(plan, later, 0, i)
        bodies.append(mine * earlier[at] + later[at])
        totals.append(mine * read_tail(plan, earlier, 0, i))
    return jnp.concatenate(bodies + [tail_rows(plan, totals)]).astype(BF16)


def group_entry(plan, total, way, turn):
    count, span = plan.seq, plan.group

    def shift(value, by):
        hop = way * by * span
        return lax.ppermute(value, "seq", [(i, (i + hop) % count) for i in range(count)])

    entry = shift(total, 1)
    by = 1
    while by < plan.groups - 1:
        entry = jnp.where(turn > by, join(plan, shift(entry, by), entry), entry)
        by *= 2
    return entry


def scan_states(plan, summaries, way):
    turn = positions(plan, way)[1]
    others = range(1, plan.group)
    got = [summaries[0]] + [swap(summaries[j], "seq", j) for j in others]
    rows, body = (plan.rows, plan.width), (plan.body, plan.width)
    pre, total = call(
        functools.partial(combine_kernel, plan, way),
        [shape((plan.group * plan.rows, plan.width), F32), shape(rows, BF16)],
        [VMEM] * plan.group,
        got,
        [pltpu.VMEM((plan.group * plan.rows, plan.width), F32)],
    )
    entry = group_entry(plan, total, way, turn)
    states = call(
        functools.partial(spread_kernel, plan, way),
        [shape(body, BF16)] * plan.group,
        [VMEM, VMEM],
        [entry, pre],
        [pltpu.VMEM((plan.group * plan.body, plan.width), BF16)],
    )
    return [states[0]] + [swap(states[j], "seq", j) for j in others]


def gather_states(plan, way, ins, scratch):
    rank = positions(plan, way)[0]
    for j in range(plan.group):
        scratch[aligned(rank ^ j, plan.body), :] = ins[j][...]


def weight_columns(offset, width):
    return aligned(lax.axis_index("head") ^ offset, width)


def grad_sum(offsets, shards, weight_ref, total=None):
    for offset, shard in zip(offsets, shards):
        part = dot(shard[...], weight_ref[:, weight_columns(offset, shard.shape[1])], 1, 1)
        total = part if total is None else total + part
    return total


def near_grad_kernel(offsets, weight_ref, *rest):
    rest[-1][...] = grad_sum(offsets, rest[:-1], weight_ref)


def grad_kernel(plan, offsets, weight_ref, *rest):
    count = len(offsets)
    shards, (part_ref, cum_ref, rise_ref, q_ref) = rest[:count], rest[count : count + 4]
    grad_ref, q_rise_ref = rest[count + 4 : count + 6]
    outs, scratch = rest[count + 6 : -1], rest[-1]
    grad_ref[...] = grad_sum(offsets, shards, weight_ref, part_ref[...]).astype(BF16)

    def cols(h):
        return slice(h * plan.width, (h + 1) * plan.width)

    def left(h):
        q_rise = (rise_ref[:, h : h + 1] * q_ref[:, cols(h)].astype(F32)).astype(BF16)
        q_rise_ref[:, cols(h)] = q_rise
        return q_rise

    rank = positions(plan, -1)[0]
    put_summaries(plan, rank, left, lambda h: grad_ref[:, cols(h)], cum_ref[...], outs, scratch)


def local_kernel(plan, cum_ref, cum_t_ref, rise_ref, fall_ref, q_ref, k_ref, v_ref, grad_ref, *outs):
    out_ref, lq_ref, lk_ref, lv_ref, g_rise_ref, v_fall_ref = outs
    scale = 1.0 / plan.width
    size = (plan.tok, plan.tok)
    lower = lax.broadcasted_iota(jnp.int32, size, 0) >= lax.broadcasted_iota(jnp.int32, size, 1)
    for h in range(plan.heads):
        at = slice(h * plan.width, (h + 1) * plan.width)
        gap = cum_ref[:, h : h + 1] - cum_t_ref[h : h + 1, :]
        mask = jnp.where(lower, jnp.exp(jnp.where(lower, gap, 0.0)), 0.0)
        q, k, v, grad = q_ref[:, at], k_ref[:, at], v_ref[:, at], grad_ref[:, at]
        attn = (scale * dot(q, k, 1, 1) * mask).astype(BF16)
        pmat = (scale * dot(grad, v, 1, 1) * mask).astype(BF16)
        out_ref[:, at] = dot(attn, v, 1, 0)
        lq_ref[:, at] = dot(pmat, k, 1, 0)
        lk_ref[:, at] = dot(pmat, q, 0, 0)
        lv_ref[:, at] = dot(attn, grad, 0, 0)
        g_rise_ref[:, at] = (rise_ref[:, h : h + 1] * grad.astype(F32)).astype(BF16)
        v_fall_ref[:, at] = (fall_ref[:, h : h + 1] * v.astype(F32)).astype(BF16)


def mix(offsets, weight_ref, flat_ref, outs):
    for offset, out in zip(offsets, outs):
        columns = weight_ref[:, weight_columns(offset, out.shape[1])]
        out[...] = dot(flat_ref[...], columns, 1, 0).astype(out.dtype)


def mix_first_kernel(plan, offsets, weight_ref, local_ref, rise_ref, *rest):
    ins, (flat_ref, *outs, states) = rest[: plan.group], rest[plan.group :]
    gather_states(plan, 1, ins, states)
    for h in range(plan.heads):
        at = slice(h * plan.width, (h + 1) * plan.width)
        cross = dot(rise_ref[:, at], states[at, :], 1, 0)
        flat_ref[:, at] = (local_ref[:, at] + cross).astype(BF16)
    mix(offsets, weight_ref, flat_ref, outs)


def near_mix_kernel(plan, offsets, weight_ref, flat_ref, lq_ref, g_rise_ref, *rest):
    ins, rest = rest[: plan.group], rest[plan.group :]
    query_grad, outs, (states, buffer, sems) = rest[0], rest[1:-3], rest[-3:]
    gather_states(plan, 1, ins, states)
    wide = plan.quarter * plan.width
    copies = []
    for h in range(plan.heads):
        at = slice(h * plan.width, (h + 1) * plan.width)
        cross = dot(g_rise_ref[:, at], states[at, :], 1, 1)
        buffer[:, at] = (lq_ref[:, at] + cross).astype(BF16)
        if (h + 1) % plan.quarter == 0:
            q = h // plan.quarter
            at = slice(q * wide, (q + 1) * wide)
            copies.append(pltpu.make_async_copy(buffer.at[:, at], query_grad.at[:, at], sems.at[q]))
            copies[-1].start()
    mix(offsets, weight_ref, flat_ref, outs)
    for copy in copies:
        copy.wait()


def last_kernel(plan, k_fall_ref, v_fall_ref, lk_ref, lv_ref, *rest):
    ins, rest = rest[: plan.group], rest[plan.group :]
    parts, (mixed, key_grad, value_grad) = rest[:3], rest[3:6]
    states, mixed_buffer, key_buffer, value_buffer, sems = rest[6:]
    copies = []

    def send(src, dst):
        copies.append(pltpu.make_async_copy(src, dst, sems.at[len(copies)]))
        copies[-1].start()

    mixed_buffer[...] = sum(part[...].astype(F32) for part in parts).astype(BF16)
    send(mixed_buffer, mixed)
    gather_states(plan, -1, ins, states)
    wide = plan.quarter * plan.width
    for h in range(plan.heads):
        at = slice(h * plan.width, (h + 1) * plan.width)
        carry = states[at, :]
        key_buffer[:, at] = (lk_ref[:, at] + dot(v_fall_ref[:, at], carry, 1, 1)).astype(BF16)
        value_buffer[:, at] = (lv_ref[:, at] + dot(k_fall_ref[:, at], carry, 1, 0)).astype(BF16)
        if (h + 1) % plan.quarter == 0:
            q = h // plan.quarter
            at = slice(q * wide, (q + 1) * wide)
            send(key_buffer.at[:, at], key_grad.at[:, at])
            send(value_buffer.at[:, at], value_grad.at[:, at])
    for copy in copies:
        copy.wait()


def local(queries, keys, values, decay_codes, out_weight, out_grad):
    tok, flat = queries.shape
    heads = decay_codes.shape[1]
    plan = Plan(tok, heads, flat // heads, lax.axis_size("seq"))
    across, feat = lax.axis_size("head"), out_grad.shape[1]
    codes = decay_codes.T
    half = across // 2
    wide = (tok, flat)

    shards = {0: out_grad}
    hop = half
    while hop:
        for o, part in list(shards.items()):
            shards[o ^ hop] = swap(part, "head", hop)
        hop //= 2

    heads_by = (tok, heads)
    weight = out_weight
    wide_bf = shape(wide, BF16)
    offsets = list(range(across))
    *summaries, cum, cum_t, rise, fall, k_fall, keys, values, queries = call(
        functools.partial(first_kernel, plan),
        summary_shapes(plan)
        + [shape(d, F32) for d in (heads_by, heads_by[::-1], heads_by, heads_by)]
        + [wide_bf] * 4,
        [HBM] * 4,
        [in_hbm(x) for x in (codes, keys, values, queries)],
        [
            summary_scratch(plan),
            pltpu.VMEM(codes.shape, codes.dtype),
            pltpu.SemaphoreType.DMA((2 * plan.group + 2,)),
        ],
    )
    states = scan_states(plan, summaries, 1)

    (part,) = call(
        functools.partial(near_grad_kernel, offsets[:half]),
        [shape(wide, F32)],
        [VMEM] * (1 + half),
        [weight] + [shards[o] for o in offsets[:half]],
    )
    grad, q_rise, *summaries_back = call(
        functools.partial(grad_kernel, plan, offsets[half:]),
        [wide_bf] * 2 + summary_shapes(plan),
        [VMEM] * (half + 5),
        [weight] + [shards[o] for o in offsets[half:]] + [part, cum, rise, queries],
        [summary_scratch(plan)],
    )
    carries = scan_states(plan, summaries_back, -1)

    local_out, local_q, local_k, local_v, g_rise, v_fall = call(
        functools.partial(local_kernel, plan),
        [shape(wide, F32)] * 4 + [wide_bf] * 2,
        [VMEM] * 8,
        [cum, cum_t, rise, fall, queries, keys, values, grad],
    )

    held = pltpu.VMEM((flat, plan.width), BF16)
    far, near = offsets[half:][::-1], offsets[:half][::-1]
    attn_out, *sent = call(
        functools.partial(mix_first_kernel, plan, far),
        [wide_bf] + [shape((tok, feat), BF16)] * half,
        [VMEM] * (3 + plan.group),
        [weight, local_out, q_rise] + states,
        [held],
    )
    query_grad, *kept = call(
        functools.partial(near_mix_kernel, plan, near),
        [wide_bf] + [shape((tok, feat), F32 if o == 0 else BF16) for o in near],
        [VMEM] * (4 + plan.group),
        [weight, attn_out, local_q, g_rise] + states,
        [held, pltpu.VMEM(wide, BF16), pltpu.SemaphoreType.DMA((plan.group,))],
        out_specs=[HBM] + [VMEM] * half,
    )

    def move(parts, hop):
        return {o: swap(part, "head", hop) for o, part in parts.items() if o & hop}

    def halve(parts, hop):
        moved = move(parts, hop)
        return {
            o: (part.astype(F32) + moved[o | hop].astype(F32)).astype(F32 if o == 0 else BF16)
            for o, part in parts.items()
            if not o & hop
        }

    far_parts, near_parts = dict(zip(far, sent)), dict(zip(near, kept))
    hop = 1
    while hop < half:
        far_parts = halve(far_parts, hop)
        if 2 * hop < half:
            near_parts = halve(near_parts, hop)
        hop *= 2
    last_parts = [near_parts[0], move(near_parts, half // 2)[half // 2], move(far_parts, half)[half]]

    mixed, key_grad, value_grad = call(
        functools.partial(last_kernel, plan),
        [shape((tok, feat), BF16)] + [wide_bf] * 2,
        [VMEM] * (7 + plan.group),
        [k_fall, v_fall, local_k, local_v] + carries + last_parts,
        [held, pltpu.VMEM((tok, feat), BF16)]
        + [pltpu.VMEM(wide, BF16)] * 2
        + [pltpu.SemaphoreType.DMA((2 * plan.group + 1,))],
        out_specs=[HBM] * 3,
    )
    return mixed, query_grad, key_grad, value_grad


def solution(mesh):
    whole = P("seq", "head")

    return jax.shard_map(
        local,
        mesh=mesh,
        in_specs=(whole, whole, whole, whole, P("head", None), whole),
        out_specs=(whole,) * 4,
        check_vma=False,
    )
```

```python
import functools

import jax
import jax.numpy as jnp
from jax import lax
from jax.experimental import pallas as pl
from jax.experimental.pallas import tpu as pltpu
from jax.sharding import PartitionSpec as P


F32 = jnp.float32
BF16 = jnp.bfloat16
VMEM = pl.BlockSpec(memory_space=pltpu.VMEM)
SMEM = pl.BlockSpec(memory_space=pltpu.SMEM)
HBM = pl.BlockSpec(memory_space=pltpu.HBM)


def dot(a, b, ca, cb):
    return lax.dot_general(a, b, (((ca,), (cb,)), ((), ())), preferred_element_type=F32)


def aligned(index, size):
    return pl.ds(pl.multiple_of(index * size, size), size)


def call(kernel, outs, specs, args, scratch=(), limit=16, out_specs=None):
    return pl.pallas_call(
        kernel,
        out_shape=outs,
        in_specs=specs,
        out_specs=out_specs or [VMEM] * len(outs),
        scratch_shapes=list(scratch),
        compiler_params=pltpu.CompilerParams(vmem_limit_bytes=limit << 20),
        cost_estimate=pl.CostEstimate(flops=2_400_000_000, bytes_accessed=8_000_000, transcendentals=0),
    )(*args)


def shape(dims, dtype):
    return jax.ShapeDtypeStruct(dims, dtype)


def running_log(codes, lower):
    rest = jnp.log(1.0 - codes.astype(F32) / 4096.0)
    columns = rows = None
    for _ in range(3):
        part = rest.astype(BF16)
        rest = rest - part.astype(F32)
        column, row = dot(lower, part, 1, 1), dot(part, lower, 1, 1)
        columns = column if columns is None else columns + column
        rows = row if rows is None else rows + row
    return columns, rows


def positions(plan, way):
    place = lax.axis_index("seq")
    turn = place if way > 0 else plan.seq - 1 - place
    return lax.rem(turn, plan.group), lax.div(turn, plan.group)


class Plan:
    def __init__(self, tok, heads, width, seq):
        self.tok, self.heads, self.width, self.seq = tok, heads, width, seq
        self.group = next(g for g in (4, 2, 1) if heads % g == 0 and seq % g == 0)
        self.groups = seq // self.group
        self.quarter = heads // self.group
        self.half_tail = 8 * pl.cdiv(self.quarter, 8)
        self.tail = 2 * self.half_tail
        self.body = self.quarter * width
        self.rows = self.body + self.tail


def tail_rows(plan, totals):
    place = lax.broadcasted_iota(jnp.int32, (plan.tail, plan.width), 0)
    rows = jnp.zeros((plan.tail, plan.width), F32)
    for i, total in enumerate(totals):
        high = total.astype(BF16).astype(F32)
        rows = jnp.where(place == i, high, rows)
        rows = jnp.where(place == plan.half_tail + i, total - high, rows)
    return rows


def read_tail(plan, ref, base, i):
    at = base + plan.body + i
    return ref[at : at + 1, :] + ref[at + plan.half_tail : at + plan.half_tail + 1, :]


def put_summaries(plan, rank, left, right, cum, outs, scratch):
    width = plan.width
    last = jnp.exp(cum[plan.tok - 1 : plan.tok, :])
    for q in range(plan.group):
        base = q * plan.rows
        totals = []
        for i in range(plan.quarter):
            h = q * plan.quarter + i
            scratch[base + i * width : base + (i + 1) * width, :] = dot(left(h), right(h), 0, 0)
            totals.append(jnp.broadcast_to(last[:, h : h + 1], (1, width)))
        scratch[base + plan.body : base + plan.rows, :] = tail_rows(plan, totals)
    outs[0][...] = scratch[aligned(rank, plan.rows), :]
    for j in range(1, plan.group):
        outs[j][...] = scratch[aligned(rank ^ j, plan.rows), :].astype(BF16)


def summary_shapes(plan):
    rows = (plan.rows, plan.width)
    return [shape(rows, F32)] + [shape(rows, BF16)] * (plan.group - 1)


def summary_scratch(plan):
    return pltpu.VMEM((plan.group * plan.rows, plan.width), F32)


def lower_kernel(lower_ref):
    place, other = (lax.broadcasted_iota(jnp.int32, lower_ref.shape, axis) for axis in (0, 1))
    lower_ref[...] = (other <= place).astype(F32).astype(BF16)


def first_kernel(plan, lower_ref, codes_ref, k_ref, v_ref, *refs):
    outs, (cum_ref, cum_t_ref, rise_ref, fall_ref, k_fall_ref, scratch) = refs[:-6], refs[-6:]
    cum, cum_t = running_log(codes_ref[...], lower_ref[...])
    fall = jnp.exp(cum[plan.tok - 1 : plan.tok, :] - cum)
    cum_ref[...], cum_t_ref[...] = cum, cum_t
    rise_ref[...] = (1.0 / plan.width) * jnp.exp(cum)
    fall_ref[...] = fall

    def cols(h):
        return slice(h * plan.width, (h + 1) * plan.width)

    def left(h):
        k_fall = (fall[:, h : h + 1] * k_ref[:, cols(h)].astype(F32)).astype(BF16)
        k_fall_ref[:, cols(h)] = k_fall
        return k_fall

    rank = positions(plan, 1)[0]
    put_summaries(plan, rank, left, lambda h: v_ref[:, cols(h)], cum, outs, scratch)


def hold_kernel(mark_ref):
    mark_ref[...] = jnp.zeros_like(mark_ref)


def combine_kernel(plan, way, *rest):
    group, width = plan.group, plan.width
    ins, (pre_ref, total_ref, scratch) = rest[:group], rest[-3:]
    rank = positions(plan, way)[0]
    for j in range(group):
        scratch[aligned(rank ^ j, plan.rows), :] = ins[j][...].astype(F32)
    decays = []
    for i in range(plan.quarter):
        held = jnp.zeros((width, width), F32)
        decay = jnp.ones((1, width), F32)
        per_member = []
        for m in range(group):
            base = m * plan.rows
            at = slice(base + i * width, base + (i + 1) * width)
            pre_ref[at, :] = held
            per_member.append(decay)
            total = read_tail(plan, scratch, base, i)
            held = total * held + scratch[at, :]
            decay = decay * total
        decays.append(per_member + [decay])
        total_ref[i * width : (i + 1) * width, :] = held.astype(BF16)
    for m in range(group):
        base = m * plan.rows + plan.body
        pre_ref[base : base + plan.tail, :] = tail_rows(plan, [d[m] for d in decays])
    total_ref[plan.body : plan.rows, :] = tail_rows(plan, [d[group] for d in decays]).astype(BF16)


def spread_kernel(plan, way, entry_ref, pre_ref, *rest):
    group, width = plan.group, plan.width
    outs, scratch = rest[:group], rest[group]
    rank, turn = positions(plan, way)
    enters = turn > 0
    for i in range(plan.quarter):
        at = slice(i * width, (i + 1) * width)
        entry = jnp.where(enters, entry_ref[at, :].astype(F32), 0.0)
        for m in range(group):
            base = m * plan.rows
            state = read_tail(plan, pre_ref, base, i) * entry
            state = state + pre_ref[base + i * width : base + (i + 1) * width, :]
            to = m * plan.body + i * width
            scratch[to : to + width, :] = state.astype(BF16)
    for j in range(group):
        outs[j][...] = scratch[aligned(rank ^ j, plan.body), :]


def swap(value, axis, offset):
    count = lax.axis_size(axis)
    return lax.ppermute(value, axis, [(i, i ^ offset) for i in range(count)])


def join(plan, earlier, later):
    earlier, later = earlier.astype(F32), later.astype(F32)
    bodies, totals = [], []
    for i in range(plan.quarter):
        at = slice(i * plan.width, (i + 1) * plan.width)
        mine = read_tail(plan, later, 0, i)
        bodies.append(mine * earlier[at] + later[at])
        totals.append(mine * read_tail(plan, earlier, 0, i))
    return jnp.concatenate(bodies + [tail_rows(plan, totals)]).astype(BF16)


def group_entry(plan, total, way, turn):
    count, span = plan.seq, plan.group

    def shift(value, by):
        hop = way * by * span
        return lax.ppermute(value, "seq", [(i, (i + hop) % count) for i in range(count)])

    entry = shift(total, 1)
    by = 1
    while by < plan.groups - 1:
        entry = jnp.where(turn > by, join(plan, shift(entry, by), entry), entry)
        by *= 2
    return entry


def scan_states(plan, summaries, way):
    turn = positions(plan, way)[1]
    others = range(1, plan.group)
    got = [summaries[0]] + [swap(summaries[j], "seq", j) for j in others]
    rows, body = (plan.rows, plan.width), (plan.body, plan.width)
    mark = call(hold_kernel, [shape((8, 128), F32)], [], [])
    pre, total = call(
        functools.partial(combine_kernel, plan, way),
        [shape((plan.group * plan.rows, plan.width), F32), shape(rows, BF16)],
        [VMEM] * (plan.group + 1),
        got + list(mark),
        [pltpu.VMEM((plan.group * plan.rows, plan.width), F32)],
    )
    entry = group_entry(plan, total, way, turn)
    states = call(
        functools.partial(spread_kernel, plan, way),
        [shape(body, BF16)] * plan.group,
        [VMEM, VMEM],
        [entry, pre],
        [pltpu.VMEM((plan.group * plan.body, plan.width), BF16)],
    )
    return [states[0]] + [swap(states[j], "seq", j) for j in others]


def gather_states(plan, way, ins, scratch):
    rank = positions(plan, way)[0]
    for j in range(plan.group):
        scratch[aligned(rank ^ j, plan.body), :] = ins[j][...]


def weight_columns(offset, width):
    return aligned(lax.axis_index("head") ^ offset, width)


def grad_sum(offsets, shards, weight_ref, total=None):
    for offset, shard in zip(offsets, shards):
        part = dot(shard[...], weight_ref[:, weight_columns(offset, shard.shape[1])], 1, 1)
        total = part if total is None else total + part
    return total


def near_grad_kernel(offsets, weight_ref, *rest):
    rest[-1][...] = grad_sum(offsets, rest[:-1], weight_ref)


def grad_kernel(plan, offsets, weight_ref, *rest):
    count = len(offsets)
    shards, (part_ref, cum_ref, rise_ref, q_ref) = rest[:count], rest[count : count + 4]
    grad_ref, q_rise_ref = rest[count + 4 : count + 6]
    outs, scratch = rest[count + 6 : -1], rest[-1]
    grad_ref[...] = grad_sum(offsets, shards, weight_ref, part_ref[...]).astype(BF16)

    def cols(h):
        return slice(h * plan.width, (h + 1) * plan.width)

    def left(h):
        q_rise = (rise_ref[:, h : h + 1] * q_ref[:, cols(h)].astype(F32)).astype(BF16)
        q_rise_ref[:, cols(h)] = q_rise
        return q_rise

    rank = positions(plan, -1)[0]
    put_summaries(plan, rank, left, lambda h: grad_ref[:, cols(h)], cum_ref[...], outs, scratch)


def local_kernel(plan, cum_ref, cum_t_ref, rise_ref, fall_ref, q_ref, k_ref, v_ref, grad_ref, *outs):
    out_ref, lq_ref, lk_ref, lv_ref, g_rise_ref, v_fall_ref = outs
    scale = 1.0 / plan.width
    size = (plan.tok, plan.tok)
    lower = lax.broadcasted_iota(jnp.int32, size, 0) >= lax.broadcasted_iota(jnp.int32, size, 1)
    for h in range(plan.heads):
        at = slice(h * plan.width, (h + 1) * plan.width)
        gap = cum_ref[:, h : h + 1] - cum_t_ref[h : h + 1, :]
        mask = jnp.where(lower, jnp.exp(jnp.where(lower, gap, 0.0)), 0.0)
        q, k, v, grad = q_ref[:, at], k_ref[:, at], v_ref[:, at], grad_ref[:, at]
        attn = (scale * dot(q, k, 1, 1) * mask).astype(BF16)
        pmat = (scale * dot(grad, v, 1, 1) * mask).astype(BF16)
        out_ref[:, at] = dot(attn, v, 1, 0)
        lq_ref[:, at] = dot(pmat, k, 1, 0)
        lk_ref[:, at] = dot(pmat, q, 0, 0)
        lv_ref[:, at] = dot(attn, grad, 0, 0)
        g_rise_ref[:, at] = (rise_ref[:, h : h + 1] * grad.astype(F32)).astype(BF16)
        v_fall_ref[:, at] = (fall_ref[:, h : h + 1] * v.astype(F32)).astype(BF16)


def mix(offsets, weight_ref, flat_ref, outs):
    for offset, out in zip(offsets, outs):
        columns = weight_ref[:, weight_columns(offset, out.shape[1])]
        out[...] = dot(flat_ref[...], columns, 1, 0).astype(out.dtype)


def mix_first_kernel(plan, offsets, weight_ref, local_ref, rise_ref, *rest):
    ins, (flat_ref, *outs, states) = rest[: plan.group], rest[plan.group :]
    gather_states(plan, 1, ins, states)
    for h in range(plan.heads):
        at = slice(h * plan.width, (h + 1) * plan.width)
        cross = dot(rise_ref[:, at], states[at, :], 1, 0)
        flat_ref[:, at] = (local_ref[:, at] + cross).astype(BF16)
    mix(offsets, weight_ref, flat_ref, outs)


def near_mix_kernel(plan, offsets, weight_ref, flat_ref, lq_ref, g_rise_ref, *rest):
    ins, rest = rest[: plan.group], rest[plan.group :]
    query_grad, outs, (states, buffer, sems) = rest[0], rest[1:-3], rest[-3:]
    gather_states(plan, 1, ins, states)
    wide = plan.quarter * plan.width
    copies = []
    for h in range(plan.heads):
        at = slice(h * plan.width, (h + 1) * plan.width)
        cross = dot(g_rise_ref[:, at], states[at, :], 1, 1)
        buffer[:, at] = (lq_ref[:, at] + cross).astype(BF16)
        if (h + 1) % plan.quarter == 0:
            q = h // plan.quarter
            at = slice(q * wide, (q + 1) * wide)
            copies.append(pltpu.make_async_copy(buffer.at[:, at], query_grad.at[:, at], sems.at[q]))
            copies[-1].start()
    mix(offsets, weight_ref, flat_ref, outs)
    for copy in copies:
        copy.wait()


def last_kernel(plan, k_fall_ref, v_fall_ref, lk_ref, lv_ref, *rest):
    ins, rest = rest[: plan.group], rest[plan.group :]
    parts, (mixed, key_grad, value_grad) = rest[:3], rest[3:6]
    states, mixed_buffer, key_buffer, value_buffer, sems = rest[6:]
    copies = []

    def send(src, dst):
        copies.append(pltpu.make_async_copy(src, dst, sems.at[len(copies)]))
        copies[-1].start()

    mixed_buffer[...] = sum(part[...].astype(F32) for part in parts).astype(BF16)
    send(mixed_buffer, mixed)
    gather_states(plan, -1, ins, states)
    wide = plan.quarter * plan.width
    for h in range(plan.heads):
        at = slice(h * plan.width, (h + 1) * plan.width)
        carry = states[at, :]
        key_buffer[:, at] = (lk_ref[:, at] + dot(v_fall_ref[:, at], carry, 1, 1)).astype(BF16)
        value_buffer[:, at] = (lv_ref[:, at] + dot(k_fall_ref[:, at], carry, 1, 0)).astype(BF16)
        if (h + 1) % plan.quarter == 0:
            q = h // plan.quarter
            at = slice(q * wide, (q + 1) * wide)
            send(key_buffer.at[:, at], key_grad.at[:, at])
            send(value_buffer.at[:, at], value_grad.at[:, at])
    for copy in copies:
        copy.wait()


def local(queries, keys, values, decay_codes, out_weight, out_grad):
    tok, flat = queries.shape
    heads = decay_codes.shape[1]
    plan = Plan(tok, heads, flat // heads, lax.axis_size("seq"))
    across, feat = lax.axis_size("head"), out_grad.shape[1]
    codes = decay_codes.T
    half = across // 2
    wide = (tok, flat)

    shards = {0: out_grad}
    hop = half
    while hop:
        for o, part in list(shards.items()):
            shards[o ^ hop] = swap(part, "head", hop)
        hop //= 2

    heads_by = (tok, heads)
    weight = out_weight
    wide_bf = shape(wide, BF16)
    offsets = list(range(across))
    (lower,) = call(lower_kernel, [shape((tok, tok), BF16)], [], [])
    *summaries, cum, cum_t, rise, fall, k_fall = call(
        functools.partial(first_kernel, plan),
        summary_shapes(plan)
        + [shape(d, F32) for d in (heads_by, heads_by[::-1], heads_by, heads_by)]
        + [wide_bf],
        [VMEM] * 4,
        [lower, codes, keys, values],
        [summary_scratch(plan)],
    )
    states = scan_states(plan, summaries, 1)

    (part,) = call(
        functools.partial(near_grad_kernel, offsets[:half]),
        [shape(wide, F32)],
        [VMEM] * (1 + half),
        [weight] + [shards[o] for o in offsets[:half]],
    )
    grad, q_rise, *summaries_back = call(
        functools.partial(grad_kernel, plan, offsets[half:]),
        [wide_bf] * 2 + summary_shapes(plan),
        [VMEM] * (half + 5),
        [weight] + [shards[o] for o in offsets[half:]] + [part, cum, rise, queries],
        [summary_scratch(plan)],
    )
    carries = scan_states(plan, summaries_back, -1)

    local_out, local_q, local_k, local_v, g_rise, v_fall = call(
        functools.partial(local_kernel, plan),
        [shape(wide, F32)] * 4 + [wide_bf] * 2,
        [VMEM] * 8,
        [cum, cum_t, rise, fall, queries, keys, values, grad],
    )

    held = pltpu.VMEM((flat, plan.width), BF16)
    far, near = offsets[half:][::-1], offsets[:half][::-1]
    attn_out, *sent = call(
        functools.partial(mix_first_kernel, plan, far),
        [wide_bf] + [shape((tok, feat), BF16)] * half,
        [VMEM] * (3 + plan.group),
        [weight, local_out, q_rise] + states,
        [held],
    )
    query_grad, *kept = call(
        functools.partial(near_mix_kernel, plan, near),
        [wide_bf] + [shape((tok, feat), F32 if o == 0 else BF16) for o in near],
        [VMEM] * (4 + plan.group),
        [weight, attn_out, local_q, g_rise] + states,
        [held, pltpu.VMEM(wide, BF16), pltpu.SemaphoreType.DMA((plan.group,))],
        out_specs=[HBM] + [VMEM] * half,
    )

    def move(parts, hop):
        return {o: swap(part, "head", hop) for o, part in parts.items() if o & hop}

    def halve(parts, hop):
        moved = move(parts, hop)
        return {
            o: (part.astype(F32) + moved[o | hop].astype(F32)).astype(F32 if o == 0 else BF16)
            for o, part in parts.items()
            if not o & hop
        }

    far_parts, near_parts = dict(zip(far, sent)), dict(zip(near, kept))
    hop = 1
    while hop < half:
        far_parts = halve(far_parts, hop)
        if 2 * hop < half:
            near_parts = halve(near_parts, hop)
        hop *= 2
    last_parts = [near_parts[0], move(near_parts, half // 2)[half // 2], move(far_parts, half)[half]]

    mixed, key_grad, value_grad = call(
        functools.partial(last_kernel, plan),
        [shape((tok, feat), BF16)] + [wide_bf] * 2,
        [VMEM] * (7 + plan.group),
        [k_fall, v_fall, local_k, local_v] + carries + last_parts,
        [held, pltpu.VMEM((tok, feat), BF16)]
        + [pltpu.VMEM(wide, BF16)] * 2
        + [pltpu.SemaphoreType.DMA((2 * plan.group + 1,))],
        out_specs=[HBM] * 3,
    )
    return mixed, query_grad, key_grad, value_grad


def solution(mesh):
    whole = P("seq", "head")

    return jax.shard_map(
        local,
        mesh=mesh,
        in_specs=(whole, whole, whole, whole, P("head", None), whole),
        out_specs=(whole,) * 4,
        check_vma=False,
    )
```

```python
import functools

import jax
import jax.numpy as jnp
from jax import lax
from jax.experimental import pallas as pl
from jax.experimental.pallas import tpu as pltpu
from jax.sharding import PartitionSpec as P


F32 = jnp.float32
BF16 = jnp.bfloat16
VMEM = pl.BlockSpec(memory_space=pltpu.VMEM)
SMEM = pl.BlockSpec(memory_space=pltpu.SMEM)
HBM = pl.BlockSpec(memory_space=pltpu.HBM)


def dot(a, b, ca, cb):
    return lax.dot_general(a, b, (((ca,), (cb,)), ((), ())), preferred_element_type=F32)


def aligned(index, size):
    return pl.ds(pl.multiple_of(index * size, size), size)


def call(kernel, outs, specs, args, scratch=(), limit=16, out_specs=None):
    return pl.pallas_call(
        kernel,
        out_shape=outs,
        in_specs=specs,
        out_specs=out_specs or [VMEM] * len(outs),
        scratch_shapes=list(scratch),
        compiler_params=pltpu.CompilerParams(vmem_limit_bytes=limit << 20),
        cost_estimate=pl.CostEstimate(flops=2_400_000_000, bytes_accessed=8_000_000, transcendentals=0),
    )(*args)


def shape(dims, dtype):
    return jax.ShapeDtypeStruct(dims, dtype)


def running_log(codes, lower):
    rest = jnp.log(1.0 - codes.astype(F32) / 4096.0)
    columns = rows = None
    for _ in range(3):
        part = rest.astype(BF16)
        rest = rest - part.astype(F32)
        column, row = dot(lower, part, 1, 1), dot(part, lower, 1, 1)
        columns = column if columns is None else columns + column
        rows = row if rows is None else rows + row
    return columns, rows


def positions(plan, way):
    place = lax.axis_index("seq")
    turn = place if way > 0 else plan.seq - 1 - place
    return lax.rem(turn, plan.group), lax.div(turn, plan.group)


class Plan:
    def __init__(self, tok, heads, width, seq):
        self.tok, self.heads, self.width, self.seq = tok, heads, width, seq
        self.group = next(g for g in (4, 2, 1) if heads % g == 0 and seq % g == 0)
        self.groups = seq // self.group
        self.quarter = heads // self.group
        self.half_tail = 8 * pl.cdiv(self.quarter, 8)
        self.tail = 2 * self.half_tail
        self.body = self.quarter * width
        self.rows = self.body + self.tail


def tail_rows(plan, totals):
    place = lax.broadcasted_iota(jnp.int32, (plan.tail, plan.width), 0)
    rows = jnp.zeros((plan.tail, plan.width), F32)
    for i, total in enumerate(totals):
        high = total.astype(BF16).astype(F32)
        rows = jnp.where(place == i, high, rows)
        rows = jnp.where(place == plan.half_tail + i, total - high, rows)
    return rows


def read_tail(plan, ref, base, i):
    at = base + plan.body + i
    return ref[at : at + 1, :] + ref[at + plan.half_tail : at + plan.half_tail + 1, :]


def put_summaries(plan, rank, left, right, cum, outs, scratch):
    width = plan.width
    last = jnp.exp(cum[plan.tok - 1 : plan.tok, :])
    for q in range(plan.group):
        base = q * plan.rows
        totals = []
        for i in range(plan.quarter):
            h = q * plan.quarter + i
            scratch[base + i * width : base + (i + 1) * width, :] = dot(left(h), right(h), 0, 0)
            totals.append(jnp.broadcast_to(last[:, h : h + 1], (1, width)))
        scratch[base + plan.body : base + plan.rows, :] = tail_rows(plan, totals)
    outs[0][...] = scratch[aligned(rank, plan.rows), :]
    for j in range(1, plan.group):
        outs[j][...] = scratch[aligned(rank ^ j, plan.rows), :].astype(BF16)


def summary_shapes(plan):
    rows = (plan.rows, plan.width)
    return [shape(rows, F32)] + [shape(rows, BF16)] * (plan.group - 1)


def summary_scratch(plan):
    return pltpu.VMEM((plan.group * plan.rows, plan.width), F32)


def lower_kernel(lower_ref):
    place, other = (lax.broadcasted_iota(jnp.int32, lower_ref.shape, axis) for axis in (0, 1))
    lower_ref[...] = (other <= place).astype(F32).astype(BF16)


def first_kernel(plan, lower_ref, codes_ref, k_ref, v_ref, *refs):
    outs, (cum_ref, cum_t_ref, rise_ref, fall_ref, k_fall_ref, scratch) = refs[:-6], refs[-6:]
    cum, cum_t = running_log(codes_ref[...], lower_ref[...])
    fall = jnp.exp(cum[plan.tok - 1 : plan.tok, :] - cum)
    cum_ref[...], cum_t_ref[...] = cum, cum_t
    rise_ref[...] = (1.0 / plan.width) * jnp.exp(cum)
    fall_ref[...] = fall

    def cols(h):
        return slice(h * plan.width, (h + 1) * plan.width)

    def left(h):
        k_fall = (fall[:, h : h + 1] * k_ref[:, cols(h)].astype(F32)).astype(BF16)
        k_fall_ref[:, cols(h)] = k_fall
        return k_fall

    rank = positions(plan, 1)[0]
    put_summaries(plan, rank, left, lambda h: v_ref[:, cols(h)], cum, outs, scratch)


def hold_kernel(mark_ref):
    mark_ref[...] = jnp.zeros_like(mark_ref)


def combine_kernel(plan, way, *rest):
    group, width = plan.group, plan.width
    ins, (pre_ref, total_ref, scratch) = rest[:group], rest[-3:]
    rank = positions(plan, way)[0]
    for j in range(group):
        scratch[aligned(rank ^ j, plan.rows), :] = ins[j][...].astype(F32)
    decays = []
    for i in range(plan.quarter):
        held = jnp.zeros((width, width), F32)
        decay = jnp.ones((1, width), F32)
        per_member = []
        for m in range(group):
            base = m * plan.rows
            at = slice(base + i * width, base + (i + 1) * width)
            pre_ref[at, :] = held
            per_member.append(decay)
            total = read_tail(plan, scratch, base, i)
            held = total * held + scratch[at, :]
            decay = decay * total
        decays.append(per_member + [decay])
        total_ref[i * width : (i + 1) * width, :] = held.astype(BF16)
    for m in range(group):
        base = m * plan.rows + plan.body
        pre_ref[base : base + plan.tail, :] = tail_rows(plan, [d[m] for d in decays])
    total_ref[plan.body : plan.rows, :] = tail_rows(plan, [d[group] for d in decays]).astype(BF16)


def spread_kernel(plan, way, entry_ref, pre_ref, *rest):
    group, width = plan.group, plan.width
    outs, scratch = rest[:group], rest[group]
    rank, turn = positions(plan, way)
    enters = turn > 0
    for i in range(plan.quarter):
        at = slice(i * width, (i + 1) * width)
        entry = jnp.where(enters, entry_ref[at, :].astype(F32), 0.0)
        for m in range(group):
            base = m * plan.rows
            state = read_tail(plan, pre_ref, base, i) * entry
            state = state + pre_ref[base + i * width : base + (i + 1) * width, :]
            to = m * plan.body + i * width
            scratch[to : to + width, :] = state.astype(BF16)
    for j in range(group):
        outs[j][...] = scratch[aligned(rank ^ j, plan.body), :]


def swap(value, axis, offset):
    count = lax.axis_size(axis)
    return lax.ppermute(value, axis, [(i, i ^ offset) for i in range(count)])


def join(plan, earlier, later):
    earlier, later = earlier.astype(F32), later.astype(F32)
    bodies, totals = [], []
    for i in range(plan.quarter):
        at = slice(i * plan.width, (i + 1) * plan.width)
        mine = read_tail(plan, later, 0, i)
        bodies.append(mine * earlier[at] + later[at])
        totals.append(mine * read_tail(plan, earlier, 0, i))
    return jnp.concatenate(bodies + [tail_rows(plan, totals)]).astype(BF16)


def group_entry(plan, total, way, turn):
    count, span = plan.seq, plan.group

    def shift(value, by):
        hop = way * by * span
        return lax.ppermute(value, "seq", [(i, (i + hop) % count) for i in range(count)])

    entry = shift(total, 1)
    by = 1
    while by < plan.groups - 1:
        entry = jnp.where(turn > by, join(plan, shift(entry, by), entry), entry)
        by *= 2
    return entry


def scan_states(plan, summaries, way):
    turn = positions(plan, way)[1]
    others = range(1, plan.group)
    got = [summaries[0]] + [swap(summaries[j], "seq", j) for j in others]
    rows, body = (plan.rows, plan.width), (plan.body, plan.width)
    mark = call(hold_kernel, [shape((8, 128), F32)], [], [])
    pre, total = call(
        functools.partial(combine_kernel, plan, way),
        [shape((plan.group * plan.rows, plan.width), F32), shape(rows, BF16)],
        [VMEM] * (plan.group + 1),
        got + list(mark),
        [pltpu.VMEM((plan.group * plan.rows, plan.width), F32)],
    )
    entry = group_entry(plan, total, way, turn)
    states = call(
        functools.partial(spread_kernel, plan, way),
        [shape(body, BF16)] * plan.group,
        [VMEM, VMEM],
        [entry, pre],
        [pltpu.VMEM((plan.group * plan.body, plan.width), BF16)],
    )
    return [states[0]] + [swap(states[j], "seq", j) for j in others]


def gather_states(plan, way, ins, scratch):
    rank = positions(plan, way)[0]
    for j in range(plan.group):
        scratch[aligned(rank ^ j, plan.body), :] = ins[j][...]


def weight_columns(offset, width):
    return aligned(lax.axis_index("head") ^ offset, width)


def grad_sum(offsets, shards, weight_ref, total=None):
    for offset, shard in zip(offsets, shards):
        part = dot(shard[...], weight_ref[:, weight_columns(offset, shard.shape[1])], 1, 1)
        total = part if total is None else total + part
    return total


def near_grad_kernel(offsets, weight_ref, *rest):
    rest[-1][...] = grad_sum(offsets, rest[:-1], weight_ref)


def more_grad_kernel(offsets, weight_ref, *rest):
    rest[-1][...] = grad_sum(offsets, rest[:-2], weight_ref, rest[-2][...])


def grad_kernel(plan, offsets, weight_ref, *rest):
    count = len(offsets)
    shards, (part_ref, cum_ref, rise_ref, q_ref) = rest[:count], rest[count : count + 4]
    grad_ref, q_rise_ref = rest[count + 4 : count + 6]
    outs, scratch = rest[count + 6 : -1], rest[-1]
    grad_ref[...] = grad_sum(offsets, shards, weight_ref, part_ref[...]).astype(BF16)

    def cols(h):
        return slice(h * plan.width, (h + 1) * plan.width)

    def left(h):
        q_rise = (rise_ref[:, h : h + 1] * q_ref[:, cols(h)].astype(F32)).astype(BF16)
        q_rise_ref[:, cols(h)] = q_rise
        return q_rise

    rank = positions(plan, -1)[0]
    put_summaries(plan, rank, left, lambda h: grad_ref[:, cols(h)], cum_ref[...], outs, scratch)


def local_kernel(plan, cum_ref, cum_t_ref, rise_ref, fall_ref, q_ref, k_ref, v_ref, grad_ref, *outs):
    out_ref, lq_ref, lk_ref, lv_ref, g_rise_ref, v_fall_ref = outs
    scale = 1.0 / plan.width
    size = (plan.tok, plan.tok)
    lower = lax.broadcasted_iota(jnp.int32, size, 0) >= lax.broadcasted_iota(jnp.int32, size, 1)
    for h in range(plan.heads):
        at = slice(h * plan.width, (h + 1) * plan.width)
        gap = cum_ref[:, h : h + 1] - cum_t_ref[h : h + 1, :]
        mask = jnp.where(lower, jnp.exp(jnp.where(lower, gap, 0.0)), 0.0)
        q, k, v, grad = q_ref[:, at], k_ref[:, at], v_ref[:, at], grad_ref[:, at]
        attn = (scale * dot(q, k, 1, 1) * mask).astype(BF16)
        pmat = (scale * dot(grad, v, 1, 1) * mask).astype(BF16)
        out_ref[:, at] = dot(attn, v, 1, 0)
        lq_ref[:, at] = dot(pmat, k, 1, 0)
        lk_ref[:, at] = dot(pmat, q, 0, 0)
        lv_ref[:, at] = dot(attn, grad, 0, 0)
        g_rise_ref[:, at] = (rise_ref[:, h : h + 1] * grad.astype(F32)).astype(BF16)
        v_fall_ref[:, at] = (fall_ref[:, h : h + 1] * v.astype(F32)).astype(BF16)


def mix(offsets, weight_ref, flat_ref, outs):
    for offset, out in zip(offsets, outs):
        columns = weight_ref[:, weight_columns(offset, out.shape[1])]
        out[...] = dot(flat_ref[...], columns, 1, 0).astype(out.dtype)


def mix_first_kernel(plan, offsets, weight_ref, local_ref, rise_ref, *rest):
    ins, (flat_ref, *outs, states) = rest[: plan.group], rest[plan.group :]
    gather_states(plan, 1, ins, states)
    for h in range(plan.heads):
        at = slice(h * plan.width, (h + 1) * plan.width)
        cross = dot(rise_ref[:, at], states[at, :], 1, 0)
        flat_ref[:, at] = (local_ref[:, at] + cross).astype(BF16)
    mix(offsets, weight_ref, flat_ref, outs)


def mix_kernel(offsets, weight_ref, flat_ref, *outs):
    mix(offsets, weight_ref, flat_ref, outs)


def near_mix_kernel(plan, offsets, weight_ref, flat_ref, lq_ref, g_rise_ref, *rest):
    ins, rest = rest[: plan.group], rest[plan.group :]
    query_grad, outs, (states, buffer, sems) = rest[0], rest[1:-3], rest[-3:]
    gather_states(plan, 1, ins, states)
    wide = plan.quarter * plan.width
    copies = []
    for h in range(plan.heads):
        at = slice(h * plan.width, (h + 1) * plan.width)
        cross = dot(g_rise_ref[:, at], states[at, :], 1, 1)
        buffer[:, at] = (lq_ref[:, at] + cross).astype(BF16)
        if (h + 1) % plan.quarter == 0:
            q = h // plan.quarter
            at = slice(q * wide, (q + 1) * wide)
            copies.append(pltpu.make_async_copy(buffer.at[:, at], query_grad.at[:, at], sems.at[q]))
            copies[-1].start()
    mix(offsets, weight_ref, flat_ref, outs)
    for copy in copies:
        copy.wait()


def key_value_part(plan, members, k_fall_ref, v_fall_ref, lk_ref, lv_ref, carries, key_out, value_out):
    rank = positions(plan, -1)[0]
    for slot, j in enumerate(members):
        for i in range(plan.quarter):
            at = aligned((rank ^ j) * plan.quarter + i, plan.width)
            carry = carries[slot][i * plan.width : (i + 1) * plan.width, :]
            start = (slot * plan.quarter + i) * plan.width
            to = slice(start, start + plan.width)
            key_out[:, to] = (lk_ref[:, at] + dot(v_fall_ref[:, at], carry, 1, 1)).astype(BF16)
            value_out[:, to] = (lv_ref[:, at] + dot(k_fall_ref[:, at], carry, 1, 0)).astype(BF16)


def early_kernel(plan, members, *refs):
    key_value_part(plan, members, *refs[:4], refs[4:-2], *refs[-2:])


def last_kernel(plan, early, late, k_fall_ref, v_fall_ref, lk_ref, lv_ref, *refs):
    carries, refs = refs[: len(late)], refs[len(late) :]
    done, parts, (mixed, key_grad, value_grad) = refs[:2], refs[2:5], refs[5:8]
    mixed_buffer, key_buffer, value_buffer, sems = refs[8:]
    rank, wide = positions(plan, -1)[0], plan.quarter * plan.width
    copies = []

    def send(src, dst):
        copies.append(pltpu.make_async_copy(src, dst, sems.at[len(copies)]))
        copies[-1].start()

    def send_quarters(members, buffers):
        for slot, j in enumerate(members):
            at, to = slice(slot * wide, (slot + 1) * wide), aligned(rank ^ j, wide)
            send(buffers[0].at[:, at], key_grad.at[:, to])
            send(buffers[1].at[:, at], value_grad.at[:, to])

    send_quarters(early, done)
    mixed_buffer[...] = sum(part[...].astype(F32) for part in parts).astype(BF16)
    send(mixed_buffer, mixed)
    buffers = (key_buffer, value_buffer)
    key_value_part(plan, late, k_fall_ref, v_fall_ref, lk_ref, lv_ref, carries, *buffers)
    send_quarters(late, buffers)
    for copy in copies:
        copy.wait()


def local(queries, keys, values, decay_codes, out_weight, out_grad):
    tok, flat = queries.shape
    heads = decay_codes.shape[1]
    plan = Plan(tok, heads, flat // heads, lax.axis_size("seq"))
    across, feat = lax.axis_size("head"), out_grad.shape[1]
    codes = decay_codes.T
    half = across // 2
    wide = (tok, flat)

    shards = {0: out_grad}
    hop = half
    while hop:
        for o, part in list(shards.items()):
            shards[o ^ hop] = swap(part, "head", hop)
        hop //= 2

    heads_by = (tok, heads)
    weight = out_weight
    wide_bf = shape(wide, BF16)
    offsets = list(range(across))
    (lower,) = call(lower_kernel, [shape((tok, tok), BF16)], [], [])
    *summaries, cum, cum_t, rise, fall, k_fall = call(
        functools.partial(first_kernel, plan),
        summary_shapes(plan)
        + [shape(d, F32) for d in (heads_by, heads_by[::-1], heads_by, heads_by)]
        + [wide_bf],
        [VMEM] * 4,
        [lower, codes, keys, values],
        [summary_scratch(plan)],
    )
    states = scan_states(plan, summaries, 1)

    (part,) = call(
        functools.partial(near_grad_kernel, offsets[:half]),
        [shape(wide, F32)],
        [VMEM] * (1 + half),
        [weight] + [shards[o] for o in offsets[:half]],
    )
    (part,) = call(
        functools.partial(more_grad_kernel, [half]),
        [shape(wide, F32)],
        [VMEM] * 3,
        [weight, shards[half], part],
    )
    grad, q_rise, *summaries_back = call(
        functools.partial(grad_kernel, plan, offsets[half + 1 :]),
        [wide_bf] * 2 + summary_shapes(plan),
        [VMEM] * (half + 4),
        [weight] + [shards[o] for o in offsets[half + 1 :]] + [part, cum, rise, queries],
        [summary_scratch(plan)],
    )
    carries = scan_states(plan, summaries_back, -1)

    local_out, local_q, local_k, local_v, g_rise, v_fall = call(
        functools.partial(local_kernel, plan),
        [shape(wide, F32)] * 4 + [wide_bf] * 2,
        [VMEM] * 8,
        [cum, cum_t, rise, fall, queries, keys, values, grad],
    )

    held = pltpu.VMEM((flat, plan.width), BF16)
    far = [o for o in offsets[half:] if o & 1] + [o for o in offsets[half:] if not o & 1]
    near = [o for o in offsets[:half] if o & 1] + [o for o in offsets[:half] if not o & 1]
    odd = half // 2
    feat_bf = shape((tok, feat), BF16)
    attn_out, *sent = call(
        functools.partial(mix_first_kernel, plan, far[:odd]),
        [wide_bf] + [feat_bf] * odd,
        [VMEM] * (3 + plan.group),
        [weight, local_out, q_rise] + states,
        [held],
    )
    sent += call(
        functools.partial(mix_kernel, far[odd:]),
        [feat_bf] * (half - odd),
        [VMEM] * 2,
        [weight, attn_out],
    )
    query_grad, *kept = call(
        functools.partial(near_mix_kernel, plan, near),
        [wide_bf] + [shape((tok, feat), F32 if o == 0 else BF16) for o in near],
        [VMEM] * (4 + plan.group),
        [weight, attn_out, local_q, g_rise] + states,
        [held, pltpu.VMEM(wide, BF16), pltpu.SemaphoreType.DMA((plan.group,))],
        out_specs=[HBM] + [VMEM] * half,
    )

    def move(parts, hop):
        return {o: swap(part, "head", hop) for o, part in parts.items() if o & hop}

    def halve(parts, hop):
        moved = move(parts, hop)
        return {
            o: (part.astype(F32) + moved[o | hop].astype(F32)).astype(F32 if o == 0 else BF16)
            for o, part in parts.items()
            if not o & hop
        }

    far_parts, near_parts = dict(zip(far, sent)), dict(zip(near, kept))
    hop = 1
    while hop < half:
        far_parts = halve(far_parts, hop)
        if 2 * hop < half:
            near_parts = halve(near_parts, hop)
        hop *= 2
    last_parts = [near_parts[0], move(near_parts, half // 2)[half // 2], move(far_parts, half)[half]]

    early = sorted({0, plan.group - 1})
    late = [j for j in range(plan.group) if j not in early]
    piece = plan.quarter * plan.width
    falls = [k_fall, v_fall, local_k, local_v]
    done = call(
        functools.partial(early_kernel, plan, early),
        [shape((tok, len(early) * piece), BF16)] * 2,
        [VMEM] * (4 + len(early)),
        falls + [carries[j] for j in early],
    )
    mixed, key_grad, value_grad = call(
        functools.partial(last_kernel, plan, early, late),
        [shape((tok, feat), BF16)] + [wide_bf] * 2,
        [VMEM] * (9 + len(late)),
        falls + [carries[j] for j in late] + list(done) + last_parts,
        [pltpu.VMEM((tok, feat), BF16)]
        + [pltpu.VMEM((tok, max(1, len(late)) * piece), BF16)] * 2
        + [pltpu.SemaphoreType.DMA((2 * plan.group + 1,))],
        out_specs=[HBM] * 3,
    )
    return mixed, query_grad, key_grad, value_grad


def solution(mesh):
    whole = P("seq", "head")

    return jax.shard_map(
        local,
        mesh=mesh,
        in_specs=(whole, whole, whole, whole, P("head", None), whole),
        out_specs=(whole,) * 4,
        check_vma=False,
    )
```

```python
import functools

import jax
import jax.numpy as jnp
from jax import lax
from jax.experimental import pallas as pl
from jax.experimental.pallas import tpu as pltpu
from jax.sharding import PartitionSpec as P


F32 = jnp.float32
BF16 = jnp.bfloat16
VMEM = pl.BlockSpec(memory_space=pltpu.VMEM)
SMEM = pl.BlockSpec(memory_space=pltpu.SMEM)
HBM = pl.BlockSpec(memory_space=pltpu.HBM)


def dot(a, b, ca, cb):
    return lax.dot_general(a, b, (((ca,), (cb,)), ((), ())), preferred_element_type=F32)


def aligned(index, size):
    return pl.ds(pl.multiple_of(index * size, size), size)


def call(kernel, outs, specs, args, scratch=(), limit=16, out_specs=None):
    return pl.pallas_call(
        kernel,
        out_shape=outs,
        in_specs=specs,
        out_specs=out_specs or [VMEM] * len(outs),
        scratch_shapes=list(scratch),
        compiler_params=pltpu.CompilerParams(vmem_limit_bytes=limit << 20),
        cost_estimate=pl.CostEstimate(flops=2_400_000_000, bytes_accessed=8_000_000, transcendentals=0),
    )(*args)


def shape(dims, dtype):
    return jax.ShapeDtypeStruct(dims, dtype)


def running_log(codes, lower):
    rest = jnp.log(1.0 - codes.astype(F32) / 4096.0)
    columns = rows = None
    for _ in range(3):
        part = rest.astype(BF16)
        rest = rest - part.astype(F32)
        column, row = dot(lower, part, 1, 1), dot(part, lower, 1, 1)
        columns = column if columns is None else columns + column
        rows = row if rows is None else rows + row
    return columns, rows


def positions(plan, way):
    place = lax.axis_index("seq")
    turn = place if way > 0 else plan.seq - 1 - place
    return lax.rem(turn, plan.group), lax.div(turn, plan.group)


class Plan:
    def __init__(self, tok, heads, width, seq):
        self.tok, self.heads, self.width, self.seq = tok, heads, width, seq
        self.group = next(g for g in (4, 2, 1) if heads % g == 0 and seq % g == 0)
        self.groups = seq // self.group
        self.quarter = heads // self.group
        self.half_tail = 8 * pl.cdiv(self.quarter, 8)
        self.tail = 2 * self.half_tail
        self.body = self.quarter * width
        self.rows = self.body + self.tail


def tail_rows(plan, totals):
    place = lax.broadcasted_iota(jnp.int32, (plan.tail, plan.width), 0)
    rows = jnp.zeros((plan.tail, plan.width), F32)
    for i, total in enumerate(totals):
        high = total.astype(BF16).astype(F32)
        rows = jnp.where(place == i, high, rows)
        rows = jnp.where(place == plan.half_tail + i, total - high, rows)
    return rows


def read_tail(plan, ref, base, i):
    at = base + plan.body + i
    return ref[at : at + 1, :] + ref[at + plan.half_tail : at + plan.half_tail + 1, :]


def put_summaries(plan, rank, left, right, cum, outs, scratch):
    width = plan.width
    last = jnp.exp(cum[plan.tok - 1 : plan.tok, :])
    for q in range(plan.group):
        base = q * plan.rows
        totals = []
        for i in range(plan.quarter):
            h = q * plan.quarter + i
            scratch[base + i * width : base + (i + 1) * width, :] = dot(left(h), right(h), 0, 0)
            totals.append(jnp.broadcast_to(last[:, h : h + 1], (1, width)))
        scratch[base + plan.body : base + plan.rows, :] = tail_rows(plan, totals)
    outs[0][...] = scratch[aligned(rank, plan.rows), :]
    for j in range(1, plan.group):
        outs[j][...] = scratch[aligned(rank ^ j, plan.rows), :].astype(BF16)


def summary_shapes(plan):
    rows = (plan.rows, plan.width)
    return [shape(rows, F32)] + [shape(rows, BF16)] * (plan.group - 1)


def summary_scratch(plan):
    return pltpu.VMEM((plan.group * plan.rows, plan.width), F32)


def lower_kernel(lower_ref):
    place, other = (lax.broadcasted_iota(jnp.int32, lower_ref.shape, axis) for axis in (0, 1))
    lower_ref[...] = (other <= place).astype(F32).astype(BF16)


def first_kernel(plan, lower_ref, codes_ref, k_ref, v_ref, *refs):
    outs, (cum_ref, cum_t_ref, rise_ref, fall_ref, k_fall_ref, scratch) = refs[:-6], refs[-6:]
    cum, cum_t = running_log(codes_ref[...], lower_ref[...])
    fall = jnp.exp(cum[plan.tok - 1 : plan.tok, :] - cum)
    cum_ref[...], cum_t_ref[...] = cum, cum_t
    rise_ref[...] = (1.0 / plan.width) * jnp.exp(cum)
    fall_ref[...] = fall

    def cols(h):
        return slice(h * plan.width, (h + 1) * plan.width)

    def left(h):
        k_fall = (fall[:, h : h + 1] * k_ref[:, cols(h)].astype(F32)).astype(BF16)
        k_fall_ref[:, cols(h)] = k_fall
        return k_fall

    rank = positions(plan, 1)[0]
    put_summaries(plan, rank, left, lambda h: v_ref[:, cols(h)], cum, outs, scratch)


def hold_kernel(mark_ref):
    mark_ref[...] = jnp.zeros_like(mark_ref)


def combine_kernel(plan, way, *rest):
    group, width = plan.group, plan.width
    ins, (pre_ref, total_ref, scratch) = rest[:group], rest[-3:]
    rank = positions(plan, way)[0]
    for j in range(group):
        scratch[aligned(rank ^ j, plan.rows), :] = ins[j][...].astype(F32)
    decays = []
    for i in range(plan.quarter):
        held = jnp.zeros((width, width), F32)
        decay = jnp.ones((1, width), F32)
        per_member = []
        for m in range(group):
            base = m * plan.rows
            at = slice(base + i * width, base + (i + 1) * width)
            pre_ref[at, :] = held
            per_member.append(decay)
            total = read_tail(plan, scratch, base, i)
            held = total * held + scratch[at, :]
            decay = decay * total
        decays.append(per_member + [decay])
        total_ref[i * width : (i + 1) * width, :] = held.astype(BF16)
    for m in range(group):
        base = m * plan.rows + plan.body
        pre_ref[base : base + plan.tail, :] = tail_rows(plan, [d[m] for d in decays])
    total_ref[plan.body : plan.rows, :] = tail_rows(plan, [d[group] for d in decays]).astype(BF16)


def spread_kernel(plan, way, entry_ref, pre_ref, *rest):
    group, width = plan.group, plan.width
    outs, scratch = rest[:group], rest[group]
    rank, turn = positions(plan, way)
    enters = turn > 0
    for i in range(plan.quarter):
        at = slice(i * width, (i + 1) * width)
        entry = jnp.where(enters, entry_ref[at, :].astype(F32), 0.0)
        for m in range(group):
            base = m * plan.rows
            state = read_tail(plan, pre_ref, base, i) * entry
            state = state + pre_ref[base + i * width : base + (i + 1) * width, :]
            to = m * plan.body + i * width
            scratch[to : to + width, :] = state.astype(BF16)
    for j in range(group):
        outs[j][...] = scratch[aligned(rank ^ j, plan.body), :]


def swap(value, axis, offset):
    count = lax.axis_size(axis)
    return lax.ppermute(value, axis, [(i, i ^ offset) for i in range(count)])


def join(plan, earlier, later):
    earlier, later = earlier.astype(F32), later.astype(F32)
    bodies, totals = [], []
    for i in range(plan.quarter):
        at = slice(i * plan.width, (i + 1) * plan.width)
        mine = read_tail(plan, later, 0, i)
        bodies.append(mine * earlier[at] + later[at])
        totals.append(mine * read_tail(plan, earlier, 0, i))
    return jnp.concatenate(bodies + [tail_rows(plan, totals)]).astype(BF16)


def group_entry(plan, total, way, turn):
    count, span = plan.seq, plan.group

    def shift(value, by):
        hop = way * by * span
        return lax.ppermute(value, "seq", [(i, (i + hop) % count) for i in range(count)])

    entry = shift(total, 1)
    by = 1
    while by < plan.groups - 1:
        entry = jnp.where(turn > by, join(plan, shift(entry, by), entry), entry)
        by *= 2
    return entry


def scan_states(plan, summaries, way):
    turn = positions(plan, way)[1]
    others = range(1, plan.group)
    got = [summaries[0]] + [swap(summaries[j], "seq", j) for j in others]
    rows, body = (plan.rows, plan.width), (plan.body, plan.width)
    mark = call(hold_kernel, [shape((8, 128), F32)], [], [])
    pre, total = call(
        functools.partial(combine_kernel, plan, way),
        [shape((plan.group * plan.rows, plan.width), F32), shape(rows, BF16)],
        [VMEM] * (plan.group + 1),
        got + list(mark),
        [pltpu.VMEM((plan.group * plan.rows, plan.width), F32)],
    )
    entry = group_entry(plan, total, way, turn)
    states = call(
        functools.partial(spread_kernel, plan, way),
        [shape(body, BF16)] * plan.group,
        [VMEM, VMEM],
        [entry, pre],
        [pltpu.VMEM((plan.group * plan.body, plan.width), BF16)],
    )
    return [states[0]] + [swap(states[j], "seq", j) for j in others]


def gather_states(plan, way, ins, scratch):
    rank = positions(plan, way)[0]
    for j in range(plan.group):
        scratch[aligned(rank ^ j, plan.body), :] = ins[j][...]


def weight_columns(offset, width):
    return aligned(lax.axis_index("head") ^ offset, width)


def grad_sum(offsets, shards, weight_ref, total=None):
    for offset, shard in zip(offsets, shards):
        part = dot(shard[...], weight_ref[:, weight_columns(offset, shard.shape[1])], 1, 1)
        total = part if total is None else total + part
    return total


def near_grad_kernel(offsets, weight_ref, *rest):
    rest[-1][...] = grad_sum(offsets, rest[:-1], weight_ref)


def more_grad_kernel(offsets, weight_ref, *rest):
    rest[-1][...] = grad_sum(offsets, rest[:-2], weight_ref, rest[-2][...])


def grad_kernel(plan, offsets, weight_ref, *rest):
    count = len(offsets)
    shards, (part_ref, cum_ref, rise_ref, q_ref) = rest[:count], rest[count : count + 4]
    grad_ref, q_rise_ref = rest[count + 4 : count + 6]
    outs, scratch = rest[count + 6 : -1], rest[-1]
    grad_ref[...] = grad_sum(offsets, shards, weight_ref, part_ref[...]).astype(BF16)

    def cols(h):
        return slice(h * plan.width, (h + 1) * plan.width)

    def left(h):
        q_rise = (rise_ref[:, h : h + 1] * q_ref[:, cols(h)].astype(F32)).astype(BF16)
        q_rise_ref[:, cols(h)] = q_rise
        return q_rise

    rank = positions(plan, -1)[0]
    put_summaries(plan, rank, left, lambda h: grad_ref[:, cols(h)], cum_ref[...], outs, scratch)


def local_kernel(plan, cum_ref, cum_t_ref, q_ref, k_ref, v_ref, grad_ref, attn_ref, pmat_ref, out_ref):
    scale = 1.0 / plan.width
    size = (plan.tok, plan.tok)
    lower = lax.broadcasted_iota(jnp.int32, size, 0) >= lax.broadcasted_iota(jnp.int32, size, 1)
    for h in range(plan.heads):
        at = slice(h * plan.width, (h + 1) * plan.width)
        rows = slice(h * plan.tok, (h + 1) * plan.tok)
        gap = cum_ref[:, h : h + 1] - cum_t_ref[h : h + 1, :]
        mask = jnp.where(lower, jnp.exp(jnp.where(lower, gap, 0.0)), 0.0)
        v = v_ref[:, at]
        attn = (scale * dot(q_ref[:, at], k_ref[:, at], 1, 1) * mask).astype(BF16)
        attn_ref[rows, :] = attn
        pmat_ref[rows, :] = (scale * dot(grad_ref[:, at], v, 1, 1) * mask).astype(BF16)
        out_ref[:, at] = dot(attn, v, 1, 0)


def local_grad_kernel(plan, rise_ref, fall_ref, q_ref, k_ref, v_ref, grad_ref, attn_ref, pmat_ref, *outs):
    lq_ref, lk_ref, lv_ref, g_rise_ref, v_fall_ref = outs
    for h in range(plan.heads):
        at = slice(h * plan.width, (h + 1) * plan.width)
        rows = slice(h * plan.tok, (h + 1) * plan.tok)
        attn, pmat, grad = attn_ref[rows, :], pmat_ref[rows, :], grad_ref[:, at]
        lq_ref[:, at] = dot(pmat, k_ref[:, at], 1, 0)
        lk_ref[:, at] = dot(pmat, q_ref[:, at], 0, 0)
        lv_ref[:, at] = dot(attn, grad, 0, 0)
        g_rise_ref[:, at] = (rise_ref[:, h : h + 1] * grad.astype(F32)).astype(BF16)
        v_fall_ref[:, at] = (fall_ref[:, h : h + 1] * v_ref[:, at].astype(F32)).astype(BF16)


def mix(offsets, weight_ref, flat_ref, outs):
    for offset, out in zip(offsets, outs):
        columns = weight_ref[:, weight_columns(offset, out.shape[1])]
        out[...] = dot(flat_ref[...], columns, 1, 0).astype(out.dtype)


def mix_first_kernel(plan, offsets, weight_ref, local_ref, rise_ref, *rest):
    ins, (flat_ref, *outs, states) = rest[: plan.group], rest[plan.group :]
    gather_states(plan, 1, ins, states)
    for h in range(plan.heads):
        at = slice(h * plan.width, (h + 1) * plan.width)
        cross = dot(rise_ref[:, at], states[at, :], 1, 0)
        flat_ref[:, at] = (local_ref[:, at] + cross).astype(BF16)
    mix(offsets, weight_ref, flat_ref, outs)


def mix_kernel(offsets, weight_ref, flat_ref, *outs):
    mix(offsets, weight_ref, flat_ref, outs)


def near_mix_kernel(plan, offsets, weight_ref, flat_ref, lq_ref, g_rise_ref, *rest):
    ins, rest = rest[: plan.group], rest[plan.group :]
    query_grad, outs, (states, buffer, sems) = rest[0], rest[1:-3], rest[-3:]
    gather_states(plan, 1, ins, states)
    wide = plan.quarter * plan.width
    copies = []
    for h in range(plan.heads):
        at = slice(h * plan.width, (h + 1) * plan.width)
        cross = dot(g_rise_ref[:, at], states[at, :], 1, 1)
        buffer[:, at] = (lq_ref[:, at] + cross).astype(BF16)
        if (h + 1) % plan.quarter == 0:
            q = h // plan.quarter
            at = slice(q * wide, (q + 1) * wide)
            copies.append(pltpu.make_async_copy(buffer.at[:, at], query_grad.at[:, at], sems.at[q]))
            copies[-1].start()
    mix(offsets, weight_ref, flat_ref, outs)
    for copy in copies:
        copy.wait()


def key_value_part(plan, members, k_fall_ref, v_fall_ref, lk_ref, lv_ref, carries, key_out, value_out):
    rank = positions(plan, -1)[0]
    for slot, j in enumerate(members):
        for i in range(plan.quarter):
            at = aligned((rank ^ j) * plan.quarter + i, plan.width)
            carry = carries[slot][i * plan.width : (i + 1) * plan.width, :]
            start = (slot * plan.quarter + i) * plan.width
            to = slice(start, start + plan.width)
            key_out[:, to] = (lk_ref[:, at] + dot(v_fall_ref[:, at], carry, 1, 1)).astype(BF16)
            value_out[:, to] = (lv_ref[:, at] + dot(k_fall_ref[:, at], carry, 1, 0)).astype(BF16)


def early_kernel(plan, members, *refs):
    key_value_part(plan, members, *refs[:4], refs[4:-2], *refs[-2:])


def last_kernel(plan, early, late, k_fall_ref, v_fall_ref, lk_ref, lv_ref, *refs):
    carries, refs = refs[: len(late)], refs[len(late) :]
    done, parts, (mixed, key_grad, value_grad) = refs[:2], refs[2:5], refs[5:8]
    mixed_buffer, key_buffer, value_buffer, sems = refs[8:]
    rank, wide = positions(plan, -1)[0], plan.quarter * plan.width
    copies = []

    def send(src, dst):
        copies.append(pltpu.make_async_copy(src, dst, sems.at[len(copies)]))
        copies[-1].start()

    def send_quarters(members, buffers):
        for slot, j in enumerate(members):
            at, to = slice(slot * wide, (slot + 1) * wide), aligned(rank ^ j, wide)
            send(buffers[0].at[:, at], key_grad.at[:, to])
            send(buffers[1].at[:, at], value_grad.at[:, to])

    send_quarters(early, done)
    mixed_buffer[...] = sum(part[...].astype(F32) for part in parts).astype(BF16)
    send(mixed_buffer, mixed)
    buffers = (key_buffer, value_buffer)
    key_value_part(plan, late, k_fall_ref, v_fall_ref, lk_ref, lv_ref, carries, *buffers)
    send_quarters(late, buffers)
    for copy in copies:
        copy.wait()


def local(queries, keys, values, decay_codes, out_weight, out_grad):
    tok, flat = queries.shape
    heads = decay_codes.shape[1]
    plan = Plan(tok, heads, flat // heads, lax.axis_size("seq"))
    across, feat = lax.axis_size("head"), out_grad.shape[1]
    codes = decay_codes.T
    half = across // 2
    wide = (tok, flat)

    shards = {0: out_grad}
    hop = half
    while hop:
        for o, part in list(shards.items()):
            shards[o ^ hop] = swap(part, "head", hop)
        hop //= 2

    heads_by = (tok, heads)
    weight = out_weight
    wide_bf = shape(wide, BF16)
    offsets = list(range(across))
    (lower,) = call(lower_kernel, [shape((tok, tok), BF16)], [], [])
    *summaries, cum, cum_t, rise, fall, k_fall = call(
        functools.partial(first_kernel, plan),
        summary_shapes(plan)
        + [shape(d, F32) for d in (heads_by, heads_by[::-1], heads_by, heads_by)]
        + [wide_bf],
        [VMEM] * 4,
        [lower, codes, keys, values],
        [summary_scratch(plan)],
    )
    states = scan_states(plan, summaries, 1)

    (part,) = call(
        functools.partial(near_grad_kernel, offsets[:half]),
        [shape(wide, F32)],
        [VMEM] * (1 + half),
        [weight] + [shards[o] for o in offsets[:half]],
    )
    (part,) = call(
        functools.partial(more_grad_kernel, [half]),
        [shape(wide, F32)],
        [VMEM] * 3,
        [weight, shards[half], part],
    )
    grad, q_rise, *summaries_back = call(
        functools.partial(grad_kernel, plan, offsets[half + 1 :]),
        [wide_bf] * 2 + summary_shapes(plan),
        [VMEM] * (half + 4),
        [weight] + [shards[o] for o in offsets[half + 1 :]] + [part, cum, rise, queries],
        [summary_scratch(plan)],
    )
    carries = scan_states(plan, summaries_back, -1)

    scores = shape((heads * tok, tok), BF16)
    attn, pmat, local_out = call(
        functools.partial(local_kernel, plan),
        [scores, scores, shape(wide, F32)],
        [VMEM] * 6,
        [cum, cum_t, queries, keys, values, grad],
    )
    local_q, local_k, local_v, g_rise, v_fall = call(
        functools.partial(local_grad_kernel, plan),
        [shape(wide, F32)] * 3 + [wide_bf] * 2,
        [VMEM] * 8,
        [rise, fall, queries, keys, values, grad, attn, pmat],
    )

    held = pltpu.VMEM((flat, plan.width), BF16)
    far = [o for o in offsets[half:] if o & 1] + [o for o in offsets[half:] if not o & 1]
    near = [o for o in offsets[:half] if o & 1] + [o for o in offsets[:half] if not o & 1]
    odd = half // 2
    feat_bf = shape((tok, feat), BF16)
    attn_out, *sent = call(
        functools.partial(mix_first_kernel, plan, far[:odd]),
        [wide_bf] + [feat_bf] * odd,
        [VMEM] * (3 + plan.group),
        [weight, local_out, q_rise] + states,
        [held],
    )
    sent += call(
        functools.partial(mix_kernel, far[odd:]),
        [feat_bf] * (half - odd),
        [VMEM] * 2,
        [weight, attn_out],
    )
    query_grad, *kept = call(
        functools.partial(near_mix_kernel, plan, near),
        [wide_bf] + [shape((tok, feat), F32 if o == 0 else BF16) for o in near],
        [VMEM] * (4 + plan.group),
        [weight, attn_out, local_q, g_rise] + states,
        [held, pltpu.VMEM(wide, BF16), pltpu.SemaphoreType.DMA((plan.group,))],
        out_specs=[HBM] + [VMEM] * half,
    )

    def move(parts, hop):
        return {o: swap(part, "head", hop) for o, part in parts.items() if o & hop}

    def halve(parts, hop):
        moved = move(parts, hop)
        return {
            o: (part.astype(F32) + moved[o | hop].astype(F32)).astype(F32 if o == 0 else BF16)
            for o, part in parts.items()
            if not o & hop
        }

    far_parts, near_parts = dict(zip(far, sent)), dict(zip(near, kept))
    hop = 1
    while hop < half:
        far_parts = halve(far_parts, hop)
        if 2 * hop < half:
            near_parts = halve(near_parts, hop)
        hop *= 2
    last_parts = [near_parts[0], move(near_parts, half // 2)[half // 2], move(far_parts, half)[half]]

    early = [j for j in range(plan.group) if j != 1]
    late = [j for j in range(plan.group) if j not in early]
    piece = plan.quarter * plan.width
    falls = [k_fall, v_fall, local_k, local_v]
    done = call(
        functools.partial(early_kernel, plan, early),
        [shape((tok, len(early) * piece), BF16)] * 2,
        [VMEM] * (4 + len(early)),
        falls + [carries[j] for j in early],
    )
    mixed, key_grad, value_grad = call(
        functools.partial(last_kernel, plan, early, late),
        [shape((tok, feat), BF16)] + [wide_bf] * 2,
        [VMEM] * (9 + len(late)),
        falls + [carries[j] for j in late] + list(done) + last_parts,
        [pltpu.VMEM((tok, feat), BF16)]
        + [pltpu.VMEM((tok, max(1, len(late)) * piece), BF16)] * 2
        + [pltpu.SemaphoreType.DMA((2 * plan.group + 1,))],
        out_specs=[HBM] * 3,
    )
    return mixed, query_grad, key_grad, value_grad


def solution(mesh):
    whole = P("seq", "head")

    return jax.shard_map(
        local,
        mesh=mesh,
        in_specs=(whole, whole, whole, whole, P("head", None), whole),
        out_specs=(whole,) * 4,
        check_vma=False,
    )
```
